512 devices in a mesh: pts: 32 (over z, x_hi, core), orb: 16 (over x_lo, y).
Axes of the slice: x: 4 (x_hi: 2, x_lo: 2; x = x_hi * 2 + x_lo), y: 8, z: 8, core: 2. Of those that a mesh axis runs over, the one named last changes fastest.
Arguments:
- phi_occ: bfloat16 [3072, 2048], P('pts', 'orb'), may hold values from -0.75 to 0.75
- phi_vir: bfloat16 [3072, 20480], P('pts', 'orb'), may hold values from -0.5 to 0.5
- eps_occ: float32 [2048], P('orb'), may hold values from -1 to -0.2
- eps_vir: float32 [20480], P('orb'), may hold values from 0.02 to 1.5
- taus: float32 [2], replicated, may hold values from 0.5 to 3
- pair_mask: int32 [32, 8], P('pts'), may hold values 0 or 1
- basis: bfloat16 [3072, 4096], P('pts', 'orb'), may hold values from -0.375 to 0.375
Outputs:
- aux_response: float32 [4096, 2, 4096], P('pts', None, 'orb')
The draws below stay inside these ranges and needn't reach their ends.
All inputs are finite; a program needn't handle non-finite values. No bound on the sum of `pair_mask` on one device may be relied on, other than what follows from the above.
Results may differ from the reference program's by a relative error of at most 0.0057.
Values may be sent and summed in bfloat16 or wider, within the bound.
No kernel may reach another device: no remote copies, remote signals or barrier semaphores. Data moves between devices by JAX's collectives and lax.ppermute only.
A program may use at most 64 MiB of HBM per device.

```python
import jax
import jax.numpy as jnp
from jax import lax

NOCC = 2048
NVIR = 20480
NAUX = 4096
NOFF = 8
NTAU = 2
TILES = 32
NP = 3072


def place_ends(entries, own_key, smallest, high):
    place = [jax.random.randint(jax.random.fold_in(own_key, axis), (), 0, length) for axis, length in enumerate(entries.shape)]
    main_axis = entries.shape.index(max(entries.shape))
    next_to = place[:main_axis] + [(place[main_axis] + 1) % entries.shape[main_axis]] + place[main_axis + 1:]
    return entries.at[tuple(place)].set(smallest).at[tuple(next_to)].set(high)


def level_of(key, shape, shards, least, high):
    factor_of, own = 1.0, jax.random.fold_in(key, 6)
    for axis_at, parts in shards:
        draws = jnp.exp(jax.random.uniform(jax.random.fold_in(own, axis_at), (parts,), jnp.float32, least / len(shards), high / len(shards)))
        factor_of = factor_of * jnp.repeat(draws, shape[axis_at] // parts).reshape([-1 if axis == axis_at else 1 for axis in range(len(shape))])
    return factor_of


def bell_draw(key, shape, width, limit, cuts=(), kind=jnp.bfloat16):
    values = width * jax.random.normal(key, shape, jnp.float32)
    if cuts:
        values = values * level_of(key, shape, cuts, -0.22, 0.18)
    return jnp.clip(values, -limit, limit).astype(kind)


def setup_inputs(seed: int = 0) -> dict:
    keys = jax.random.split(jax.random.key(seed), 8)
    phi_occ = bell_draw(keys[0], (NP, NOCC), 64 ** -0.5, 0.75, ((0, 32), (1, 16)))
    phi_vir = bell_draw(keys[1], (NP, NVIR), 143 ** -0.5, 0.5, ((0, 32), (1, 16)))
    eps_occ = jnp.clip(-1.0 + 0.8 * jax.random.uniform(keys[2], (NOCC,), jnp.float32) ** level_of(keys[2], (NOCC,), ((0, 16),), -0.2, 0.2), -1.0, -0.2)
    eps_vir = jnp.clip(0.02 + 1.48 * jax.random.uniform(keys[3], (NVIR,), jnp.float32) ** level_of(keys[3], (NVIR,), ((0, 16),), -0.2, 0.2), 0.02, 1.5)
    taus = jnp.clip(jax.random.uniform(keys[4], (NTAU,), jnp.float32, 0.5, 3.0), 0.5, 3.0)
    pair_mask = place_ends((jax.random.randint(keys[5], (TILES, NOFF), 0, 4) < 3).astype(jnp.int32), jax.random.fold_in(keys[5], 1), 0, 1)
    basis = bell_draw(keys[6], (NP, NAUX), 256 ** -0.5, 0.375, ((0, 32), (1, 16)))
    return dict(phi_occ=phi_occ, phi_vir=phi_vir, eps_occ=eps_occ, eps_vir=eps_vir, taus=taus, pair_mask=pair_mask, basis=basis)


def partner_offsets(count):
    half = count // 2
    return [k - half for k in range(half)] + [k + 1 for k in range(half)]


def reference(phi_occ, phi_vir, eps_occ, eps_vir, taus, pair_mask, basis):
    tiles = pair_mask.shape[0]
    rows = phi_occ.shape[0] // tiles
    offsets = partner_offsets(pair_mask.shape[1])
    expo_occ = jnp.exp(taus[:, None] * eps_occ[None, :])
    expo_vir = jnp.exp(-taus[:, None] * eps_vir[None, :])
    weighted_occ = (phi_occ.astype(jnp.float32)[None] * expo_occ[:, None, :]).astype(jnp.bfloat16)
    weighted_vir = (phi_vir.astype(jnp.float32)[None] * expo_vir[:, None, :]).astype(jnp.bfloat16)

    def one_tile(tile):
        start = (tile * rows).astype(jnp.int32)
        own_occ = lax.dynamic_slice_in_dim(weighted_occ, start, rows, 1)
        own_vir = lax.dynamic_slice_in_dim(weighted_vir, start, rows, 1)
        totals = [jnp.zeros((rows, basis.shape[1]), jnp.float32) for t in range(taus.shape[0])]
        for k, shift in enumerate(offsets):
            other = (((tile + shift) % tiles) * rows).astype(jnp.int32)
            occ_part = lax.dynamic_slice_in_dim(phi_occ, other, rows, 0)
            vir_part = lax.dynamic_slice_in_dim(phi_vir, other, rows, 0)
            basis_part = lax.dynamic_slice_in_dim(basis, other, rows, 0)
            factor = pair_mask[tile, k].astype(jnp.float32)
            for t in range(taus.shape[0]):
                g_occ = jnp.dot(own_occ[t], occ_part.T, preferred_element_type=jnp.float32)
                g_vir = jnp.dot(own_vir[t], vir_part.T, preferred_element_type=jnp.float32)
                chi = (g_occ * g_vir * factor).astype(jnp.bfloat16)
                totals[t] = totals[t] + jnp.dot(chi, basis_part, preferred_element_type=jnp.float32)
        return jnp.stack(totals).astype(jnp.bfloat16)

    projected = lax.map(one_tile, jnp.arange(tiles, dtype=jnp.int32))
    projected = jnp.transpose(projected, (1, 0, 2, 3)).reshape(taus.shape[0], tiles * rows, basis.shape[1])
    return jnp.einsum("rp,trq->ptq", basis.astype(jnp.float32), projected.astype(jnp.float32))
```

```python
import jax
import jax.numpy as jnp
from jax import lax
from jax.sharding import Mesh, PartitionSpec as P

ORB = ("xl", "y")
PTS = ("z", "xh", "core")
BF = jnp.bfloat16
F32 = jnp.float32


def shift_tiles(value, steps):
    pairs = [((i + steps) % 32, i) for i in range(32)]
    return lax.ppermute(value, PTS, pairs)


def swap_core(value):
    return lax.ppermute(value, "core", [(0, 1), (1, 0)])


def to_all(value, axes, count):
    copies = jnp.broadcast_to(value[None], (count,) + value.shape)
    return lax.all_to_all(copies, axes, 0, 0, tiled=True)


def on_device(phi_occ, phi_vir, eps_occ, eps_vir, taus, pair_mask, basis):
    core = lax.axis_index("core")
    nocc, nvir, naux = phi_occ.shape[1], phi_vir.shape[1], basis.shape[1]
    rows = phi_occ.shape[0]
    mask = jnp.pad(pair_mask.astype(BF), ((0, 0), (0, 120)))
    mask = jnp.broadcast_to(mask, (rows, 128))
    packed = jnp.concatenate([phi_occ, phi_vir, basis], axis=1)
    moves = []
    for z in range(8):
        for o in range(16):
            moves.append((z * 16 + o, (o // 2) * 16 + z * 2 + o % 2))
    basis_part = lax.ppermute(basis, ("z", "xl", "y"), moves)
    other = swap_core(jnp.concatenate([packed, mask], axis=1))
    got = [shift_tiles(packed, d) for d in (-4, -2, 2, 4)]
    basis_cols = to_all(basis_part, ORB, 16)
    tiles = [got[0], got[1], packed, got[2], got[3]]
    own_panel = jnp.concatenate([got[0], got[1], got[2], got[3]], axis=0)
    low = jnp.concatenate([got[0], got[1], packed, got[2]], axis=0)
    high = jnp.concatenate([got[1], packed, got[2], got[3]], axis=0)
    other_panel = jnp.where(core == 0, high, low)
    mask_own = mask[0, :8].astype(F32)
    mask_other = other[0, nocc + nvir + naux : nocc + nvir + naux + 8].astype(F32)
    expo_occ = jnp.exp(taus[:, None] * eps_occ[None, :])
    expo_vir = jnp.exp(-taus[:, None] * eps_vir[None, :])
    left = jnp.stack([packed, other[:, : nocc + nvir + naux]]).astype(F32)
    w_occ = (left[None, :, :, :nocc] * expo_occ[:, None, None, :]).astype(BF)
    w_vir = (left[None, :, :, nocc : nocc + nvir] * expo_vir[:, None, None, :]).astype(BF)
    panels = jnp.stack([own_panel, other_panel])
    g_occ = jnp.einsum("tsra,sca->tsrc", w_occ, panels[:, :, :nocc], preferred_element_type=F32)
    g_vir = jnp.einsum(
        "tsra,sca->tsrc", w_vir, panels[:, :, nocc : nocc + nvir], preferred_element_type=F32
    )
    part = jnp.stack([g_occ.astype(BF), g_vir.astype(BF)], axis=3)
    part = part.reshape(16, 24, 2, 384).transpose(0, 2, 1, 3)
    recv = lax.all_to_all(part, ORB, 0, 0, tiled=True).astype(F32)
    total = recv.sum(axis=0)
    me = lax.axis_index(ORB)
    s = (me // 4) % 2
    m_own = jnp.stack([mask_own[i] for i in (0, 2, 5, 7)])
    m_other = jnp.stack([mask_other[i] for i in (1, 3, 4, 6)])
    factor = jnp.repeat(jnp.where(s == 0, m_own, m_other), 96)
    chi = (total[0] * total[1] * factor[None, :]).astype(BF)
    chi = to_all(chi, ORB, 16).reshape(2, 2, 96, 384)
    proj = jnp.einsum(
        "tsrc,scq->strq".replace(" ", ""), chi, panels[:, :, nocc + nvir :], preferred_element_type=F32
    )
    projected = (proj[0] + swap_core(proj[1])).astype(BF)
    gathered = to_all(projected, "z", 8)
    cols = basis_cols.reshape(8, 2, rows, naux)
    resp = jnp.einsum("zhrp,ztrq->hptq", cols, gathered, preferred_element_type=F32)
    resp = resp.reshape(4, 128, 2, naux).astype(BF)
    resp = lax.all_to_all(resp, ("xh", "core"), 0, 0, tiled=True)
    return resp.astype(F32).sum(axis=0)


def solution(mesh):
    names = ("z", "xh", "core", "xl", "y")
    fine = Mesh(mesh.devices.reshape(8, 2, 2, 2, 8), names)
    placed = (P(PTS, ORB), P(PTS, ORB), P(ORB), P(ORB), P(), P(PTS, None), P(PTS, ORB))
    return jax.shard_map(
        on_device, mesh=fine, in_specs=placed, out_specs=P(PTS, None, ORB), check_vma=False
    )
```

```python
import jax
import jax.numpy as jnp
from jax import lax
from jax.sharding import Mesh, PartitionSpec as P

ORB = ("xl", "y")
PTS = ("z", "xh", "core")
BF = jnp.bfloat16
F32 = jnp.float32
SWAP = [(0, 1), (1, 0)]


def from_tile(value, steps):
    return lax.ppermute(value, PTS, [((i + steps) % 32, i) for i in range(32)])


def to_all(value, axes, count):
    copies = jnp.broadcast_to(value[None], (count,) + value.shape)
    return lax.all_to_all(copies, axes, 0, 0, tiled=True)


def on_device(phi_occ, phi_vir, eps_occ, eps_vir, taus, pair_mask, basis):
    core, xl, xh = lax.axis_index("core"), lax.axis_index("xl"), lax.axis_index("xh")
    nocc, nvir, naux = phi_occ.shape[1], phi_vir.shape[1], basis.shape[1]
    rows = phi_occ.shape[0]
    ends = (nocc, nocc + nvir, nocc + nvir + naux)
    first = core == 0
    mask = jnp.pad(pair_mask.astype(BF), ((0, 0), (0, 120)))
    mine = jnp.concatenate(
        [phi_occ, phi_vir, basis, jnp.broadcast_to(mask, (rows, 128))], axis=1
    )
    up = from_tile(mine, 2)
    down = from_tile(mine, -4)
    mate = lax.ppermute(mine, "core", SWAP)
    moves = [(z * 16 + o, (o // 2) * 16 + z * 2 + o % 2) for z in range(8) for o in range(16)]
    part = lax.ppermute(basis, ("z", "xl", "y"), moves)
    near = to_all(part, "y", 8)

    fourth = jnp.where(first, mine, down)

    def masks(slab):
        return slab[0, ends[2] : ends[2] + 8].astype(F32)

    m_own, m_mate, m_up, m_down = masks(mine), masks(mate), masks(up), masks(down)
    row_mask = jnp.stack(
        [m_own[5], m_own[0], jnp.where(first, m_mate[4], m_mate[6]), jnp.where(first, m_mate[3], m_mate[1])]
    )
    col_mask = jnp.stack(
        [m_up[2], m_down[7], jnp.where(first, m_up[3], m_up[1]), jnp.where(first, m_own[4], m_down[6])]
    )
    row_mask = jnp.repeat(row_mask, rows)
    col_mask = jnp.repeat(col_mask, rows)

    expo_occ = jnp.exp(taus[:, None] * eps_occ[None, :])
    expo_vir = jnp.exp(-taus[:, None] * eps_vir[None, :])

    def weighted(slab, lo, hi, expo):
        return (slab[None, :, lo:hi].astype(F32) * expo[:, None, :]).astype(BF)

    def green(lo, hi, expo):
        a = jnp.einsum(
            "tra,ca->trc",
            weighted(mine, lo, hi, expo),
            jnp.concatenate([up[:, lo:hi], down[:, lo:hi]]),
            preferred_element_type=F32,
        )
        b = jnp.einsum(
            "tra,ca->trc",
            weighted(mate, lo, hi, expo),
            jnp.concatenate([up[:, lo:hi], fourth[:, lo:hi]]),
            preferred_element_type=F32,
        )
        return jnp.concatenate([a, b], axis=2).astype(BF).reshape(16, 12, 4 * rows)

    part_sums = jnp.concatenate(
        [green(0, ends[0], expo_occ), green(ends[0], ends[1], expo_vir)], axis=1
    )
    part_sums, near = lax.optimization_barrier((part_sums, near))
    sums = lax.all_to_all(part_sums, ORB, 0, 0, tiled=True).astype(F32).sum(axis=0)
    both = (sums[:12] * sums[12:]).astype(BF)
    far = lax.ppermute(near, "xl", SWAP)
    low = jnp.where(xl == 0, near, far)
    high = jnp.where(xl == 0, far, near)
    cols = jnp.concatenate([low, high]).reshape(8, 2, rows, naux)
    both = to_all(both, ORB, 16).reshape(2, rows, 4 * rows)
    by_row = (both.astype(F32) * row_mask).astype(BF)
    by_col = (both.astype(F32) * col_mask).astype(BF)

    def aux(slab):
        return slab[:, ends[1] : ends[2]]

    def rows_of(block, *panels):
        return jnp.einsum("trc,cq->trq", block, jnp.concatenate(panels), preferred_element_type=F32)

    def cols_of(block, panel):
        return jnp.einsum("trc,rq->tcq", block, panel, preferred_element_type=F32)

    r2, r3 = 2 * rows, 3 * rows
    to_mate = rows_of(by_row[:, :, r2:], aux(up), aux(fourth))
    to_up = cols_of(by_col[:, :, :rows], aux(mine)) + cols_of(by_col[:, :, r2:r3], aux(mate))
    last = cols_of(by_col[:, :, r3:], aux(mate))
    zero = jnp.zeros_like(last)
    to_down = cols_of(by_col[:, :, rows:r2], aux(mine)) + jnp.where(first, zero, last)
    own = rows_of(by_row[:, :, :r2], aux(up), aux(down)) + jnp.where(first, last, zero)
    got_up = from_tile(to_up.astype(BF), -2)
    got_down = from_tile(to_down.astype(BF), 4)
    got_mate = lax.ppermute(to_mate, "core", SWAP)
    projected = (own + got_mate + got_up.astype(F32) + got_down.astype(F32)).astype(BF)

    gathered = to_all(projected, "z", 8)
    at = xh * 2 + core
    blocks = cols.reshape(8, 2, rows, 2, naux // 2)

    def response(flip):
        j = at ^ flip
        chosen = lax.dynamic_slice(
            blocks, (0, j // 2, 0, j % 2, 0), (8, 1, rows, 1, naux // 2)
        ).reshape(8, rows, naux // 2)
        return jnp.einsum("zrp,ztrq->ptq", chosen, gathered, preferred_element_type=F32)

    both_way = lax.ppermute(
        response(3).astype(BF), ("xh", "core"), [(0, 3), (3, 0), (1, 2), (2, 1)]
    )
    across = lax.ppermute(response(2).astype(BF), "xh", SWAP)
    beside = lax.ppermute(response(1), "core", SWAP)
    return response(0) + beside + across.astype(F32) + both_way.astype(F32)


def solution(mesh):
    names = ("z", "xh", "core", "xl", "y")
    fine = Mesh(mesh.devices.reshape(8, 2, 2, 2, 8), names)
    placed = (P(PTS, ORB), P(PTS, ORB), P(ORB), P(ORB), P(), P(PTS, None), P(PTS, ORB))
    return jax.shard_map(
        on_device, mesh=fine, in_specs=placed, out_specs=P(PTS, None, ORB), check_vma=False
    )
```

```python
import jax
import jax.numpy as jnp
from jax import lax
from jax.experimental import pallas as pl
from jax.experimental.pallas import tpu as pltpu
from jax.sharding import Mesh, PartitionSpec as P


ORB = ("xl", "y")
PTS = ("z", "xh", "core")
BF = jnp.bfloat16
F32 = jnp.float32
SWAP = [(0, 1), (1, 0)]
LAST = (((1,), (1,)), ((), ()))
WHOLE = pl.BlockSpec(memory_space=pltpu.VMEM)
SCALARS = pl.BlockSpec(memory_space=pltpu.SMEM)


def from_tile(value, steps):
    return lax.ppermute(value, PTS, [((i + steps) % 32, i) for i in range(32)])


def trade(value, axis, bit, at):
    size = lax.axis_size(axis)
    got = lax.ppermute(value, axis, [(i, i ^ bit) for i in range(size)])
    upper = (lax.axis_index(axis) & bit) != 0
    return jnp.stack([jnp.where(upper, got, value), jnp.where(upper, value, got)], axis=at)


def to_all(value, axes, count):
    copies = jnp.broadcast_to(value[None], (count,) + value.shape)
    return lax.all_to_all(copies, axes, 0, 0, tiled=True)


def green_kernel(core, taus, eps_occ, eps_vir, mine, mate, up, down, out, panel, left, total, rows12):
    rows = mine.shape[0]
    nocc, cols = eps_occ.shape[1], mine.shape[1]
    panel[0:rows] = up[...]
    panel[rows : 2 * rows] = down[...]
    panel[2 * rows : 3 * rows] = up[...]

    @pl.when(core[0] == 0)
    def _():
        panel[3 * rows : 4 * rows] = mine[...]

    @pl.when(core[0] != 0)
    def _():
        panel[3 * rows : 4 * rows] = down[...]

    for t in range(2):
        for lo, hi, eps, sign in ((0, nocc, eps_occ, 1.0), (nocc, cols, eps_vir, -1.0)):
            expo = jnp.exp((sign * taus[t]) * eps[...])
            for s, slab in enumerate((mine, mate)):
                at = (2 * s + t) * rows
                left[at : at + rows, lo:hi] = (slab[:, lo:hi].astype(F32) * expo).astype(BF)
    lane = lax.broadcasted_iota(jnp.int32, (2 * rows, 4 * rows), 1)
    for q, (lo, hi) in enumerate(((0, nocc), (nocc, cols))):
        a = lax.dot_general(
            left[0 : 2 * rows, lo:hi], panel[:, lo:hi], LAST, preferred_element_type=F32
        )
        b = lax.dot_general(
            left[2 * rows : 4 * rows, lo:hi], panel[:, lo:hi], LAST, preferred_element_type=F32
        )
        total[q] = jnp.where(lane < 2 * rows, a, b)
    for j in range(16):
        rows12[j, 0:12] = total[0, 12 * j : 12 * j + 12]
        rows12[j, 12:24] = total[1, 12 * j : 12 * j + 12]
    out[...] = rows12[...].astype(BF)


def green(core, taus, eps_occ, eps_vir, mine, mate, up, down):
    rows, cols = mine.shape
    return pl.pallas_call(
        green_kernel,
        out_shape=jax.ShapeDtypeStruct((16, 24, 4 * rows), BF),
        in_specs=[SCALARS, SCALARS] + [WHOLE] * 6,
        out_specs=WHOLE,
        scratch_shapes=[
            pltpu.VMEM((4 * rows, cols), BF),
            pltpu.VMEM((4 * rows, cols), BF),
            pltpu.VMEM((2, 2 * rows, 4 * rows), F32),
            pltpu.VMEM((16, 24, 4 * rows), F32),
        ],
        compiler_params=pltpu.CompilerParams(vmem_limit_bytes=16 * 2**20),
        cost_estimate=pl.CostEstimate(
            flops=8 * rows * 4 * rows * cols, bytes_accessed=10 * rows * cols, transcendentals=4 * cols
        ),
        name="green",
    )(core, taus, eps_occ, eps_vir, mine, mate, up, down)


def product_kernel(parts, out, total):
    total[...] = parts[...].astype(F32).sum(axis=0)
    both = (total[0:12] * total[12:24]).astype(BF)
    for j in range(16):
        out[j] = both


def product(parts):
    return pl.pallas_call(
        product_kernel,
        out_shape=jax.ShapeDtypeStruct((16, 12, parts.shape[2]), BF),
        in_specs=[WHOLE],
        out_specs=WHOLE,
        scratch_shapes=[pltpu.VMEM(parts.shape[1:], F32)],
        compiler_params=pltpu.CompilerParams(vmem_limit_bytes=8 * 2**20),
        cost_estimate=pl.CostEstimate(
            flops=parts.size, bytes_accessed=4 * parts.size, transcendentals=0
        ),
        name="product",
    )(parts)


def on_device(phi_occ, phi_vir, eps_occ, eps_vir, taus, pair_mask, basis):
    core, xh = lax.axis_index("core"), lax.axis_index("xh")
    naux, rows = basis.shape[1], phi_occ.shape[0]
    first = core == 0
    mine = jnp.concatenate([phi_occ, phi_vir], axis=1)
    up = from_tile(mine, 2)
    down = from_tile(mine, -4)
    mate = lax.ppermute(mine, "core", SWAP)
    moves = [(z * 16 + o, (o // 2) * 16 + z * 2 + o % 2) for z in range(8) for o in range(16)]
    part = lax.ppermute(basis, ("z", "xl", "y"), moves)
    mask = jnp.pad(pair_mask.astype(BF), ((0, 0), (0, 120)))
    extra = jnp.concatenate([basis, jnp.broadcast_to(mask, (rows, 128))], axis=1)

    part_sums = green(
        core.reshape(1), taus, eps_occ[None], eps_vir[None], mine, mate, up, down
    )
    part_sums, extra, part = lax.optimization_barrier((part_sums, extra, part))
    sums = lax.all_to_all(part_sums, ORB, 0, 0, tiled=True)
    x_up = from_tile(extra, 2)
    x_down = from_tile(extra, -4)
    x_mate = lax.ppermute(extra, "core", SWAP)
    part = trade(part, "y", 4, 0)
    x_fourth = jnp.where(first, extra, x_down)

    def masks(slab):
        return slab[0, naux : naux + 8].astype(F32)

    m_own, m_mate, m_up, m_down = masks(extra), masks(x_mate), masks(x_up), masks(x_down)
    row_mask = jnp.stack(
        [m_own[5], m_own[0], jnp.where(first, m_mate[4], m_mate[6]), jnp.where(first, m_mate[3], m_mate[1])]
    )
    col_mask = jnp.stack(
        [m_up[2], m_down[7], jnp.where(first, m_up[3], m_up[1]), jnp.where(first, m_own[4], m_down[6])]
    )
    row_mask = jnp.repeat(row_mask, rows)
    col_mask = jnp.repeat(col_mask, rows)

    both = product(sums)
    both, part = lax.optimization_barrier((both, part))
    both = lax.all_to_all(both, ORB, 0, 0, tiled=True).reshape(2, rows, 4 * rows)
    part = trade(part, "y", 2, 1)
    by_row = (both.astype(F32) * row_mask).astype(BF)
    by_col = (both.astype(F32) * col_mask).astype(BF)

    def aux(slab):
        return slab[:, :naux]

    def rows_of(block, *panels):
        return jnp.einsum("trc,cq->trq", block, jnp.concatenate(panels), preferred_element_type=F32)

    def cols_of(block, panel):
        return jnp.einsum("trc,rq->tcq", block, panel, preferred_element_type=F32)

    r2, r3 = 2 * rows, 3 * rows
    to_up = cols_of(by_col[:, :, :rows], aux(extra)) + cols_of(by_col[:, :, r2:r3], aux(x_mate))
    last = cols_of(by_col[:, :, r3:], aux(x_mate))
    zero = jnp.zeros_like(last)
    to_down = cols_of(by_col[:, :, rows:r2], aux(extra)) + jnp.where(first, zero, last)
    to_mate = rows_of(by_row[:, :, r2:], aux(x_up), aux(x_fourth))
    own = rows_of(by_row[:, :, :r2], aux(x_up), aux(x_down)) + jnp.where(first, last, zero)
    to_up, part = lax.optimization_barrier((to_up.astype(BF), part))
    got_up = from_tile(to_up, -2)
    got_down = from_tile(to_down.astype(BF), 4)
    got_mate = lax.ppermute(to_mate, "core", SWAP)
    part = trade(part, "y", 1, 0)
    projected = (own + got_mate + got_up.astype(F32) + got_down.astype(F32)).astype(BF)

    projected, part = lax.optimization_barrier((projected, part))
    gathered = to_all(projected, "z", 8)
    part = trade(part, "xl", 1, 1)
    blocks = part.reshape(2, 8, rows, naux)
    at = xh * 2 + core

    def response(flip):
        j = at ^ flip
        chosen = lax.dynamic_slice(
            blocks, (j // 2, 0, 0, (j % 2) * (naux // 2)), (1, 8, rows, naux // 2)
        )[0]
        return jnp.einsum("zrp,ztrq->ptq", chosen, gathered, preferred_element_type=F32)

    both_way = lax.ppermute(
        response(3).astype(BF), ("xh", "core"), [(0, 3), (3, 0), (1, 2), (2, 1)]
    )
    across = lax.ppermute(response(2).astype(BF), "xh", SWAP)
    beside = lax.ppermute(response(1), "core", SWAP)
    return response(0) + beside + across.astype(F32) + both_way.astype(F32)


def solution(mesh):
    names = ("z", "xh", "core", "xl", "y")
    fine = Mesh(mesh.devices.reshape(8, 2, 2, 2, 8), names)
    placed = (P(PTS, ORB), P(PTS, ORB), P(ORB), P(ORB), P(), P(PTS, None), P(PTS, ORB))

    return jax.shard_map(
        on_device, mesh=fine, in_specs=placed, out_specs=P(PTS, None, ORB), check_vma=False
    )
```

```python
import jax
import jax.numpy as jnp
from jax import lax
from jax.experimental import pallas as pl
from jax.experimental.pallas import tpu as pltpu
from jax.sharding import Mesh, PartitionSpec as P


ORB = ("xl", "y")
PTS = ("z", "xh", "core")
BF = jnp.bfloat16
F32 = jnp.float32
SWAP = [(0, 1), (1, 0)]
LAST = (((1,), (1,)), ((), ()))
WHOLE = pl.BlockSpec(memory_space=pltpu.VMEM)
SCALARS = pl.BlockSpec(memory_space=pltpu.SMEM)


def from_tile(value, steps):
    return lax.ppermute(value, PTS, [((i + steps) % 32, i) for i in range(32)])


def trade(value, axis, bit):
    size = lax.axis_size(axis)
    return lax.ppermute(value, axis, [(i, i ^ bit) for i in range(size)])


def join(value, got, axis, bit, at):
    upper = (lax.axis_index(axis) & bit) != 0
    return jnp.stack([jnp.where(upper, got, value), jnp.where(upper, value, got)], axis=at)


def to_all(value, axes, count):
    copies = jnp.broadcast_to(value[None], (count,) + value.shape)
    return lax.all_to_all(copies, axes, 0, 0, tiled=True)


def green_kernel(core, taus, eps_occ, eps_vir, mine, mate, up, down, out, panel, left, total, rows12):
    rows = mine.shape[0]
    nocc, cols = eps_occ.shape[1], eps_occ.shape[1] + eps_vir.shape[1]
    panel[0:rows] = up[:, :cols]
    panel[rows : 2 * rows] = down[:, :cols]
    panel[2 * rows : 3 * rows] = up[:, :cols]

    @pl.when(core[0] == 0)
    def _():
        panel[3 * rows : 4 * rows] = mine[:, :cols]

    @pl.when(core[0] != 0)
    def _():
        panel[3 * rows : 4 * rows] = down[:, :cols]

    for t in range(2):
        for lo, hi, eps, sign in ((0, nocc, eps_occ, 1.0), (nocc, cols, eps_vir, -1.0)):
            expo = jnp.exp((sign * taus[t]) * eps[...])
            for s, slab in enumerate((mine, mate)):
                at = (2 * s + t) * rows
                left[at : at + rows, lo:hi] = (slab[:, lo:hi].astype(F32) * expo).astype(BF)
    lane = lax.broadcasted_iota(jnp.int32, (2 * rows, 4 * rows), 1)
    for q, (lo, hi) in enumerate(((0, nocc), (nocc, cols))):
        a = lax.dot_general(
            left[0 : 2 * rows, lo:hi], panel[:, lo:hi], LAST, preferred_element_type=F32
        )
        b = lax.dot_general(
            left[2 * rows : 4 * rows, lo:hi], panel[:, lo:hi], LAST, preferred_element_type=F32
        )
        total[q] = jnp.where(lane < 2 * rows, a, b)
    for j in range(16):
        rows12[j, 0:12] = total[0, 12 * j : 12 * j + 12]
        rows12[j, 12:24] = total[1, 12 * j : 12 * j + 12]
    out[...] = rows12[...].astype(BF)


def green(core, taus, eps_occ, eps_vir, mine, mate, up, down):
    rows, cols = mine.shape[0], eps_occ.shape[1] + eps_vir.shape[1]
    return pl.pallas_call(
        green_kernel,
        out_shape=jax.ShapeDtypeStruct((16, 24, 4 * rows), BF),
        in_specs=[SCALARS, SCALARS] + [WHOLE] * 6,
        out_specs=WHOLE,
        scratch_shapes=[
            pltpu.VMEM((4 * rows, cols), BF),
            pltpu.VMEM((4 * rows, cols), BF),
            pltpu.VMEM((2, 2 * rows, 4 * rows), F32),
            pltpu.VMEM((16, 24, 4 * rows), F32),
        ],
        compiler_params=pltpu.CompilerParams(vmem_limit_bytes=16 * 2**20),
        cost_estimate=pl.CostEstimate(
            flops=8 * rows * 4 * rows * cols, bytes_accessed=10 * rows * cols, transcendentals=4 * cols
        ),
        name="green",
    )(core, taus, eps_occ, eps_vir, mine, mate, up, down)


def product_kernel(parts, out, total):
    total[...] = parts[...].astype(F32).sum(axis=0)
    both = (total[0:12] * total[12:24]).astype(BF)
    for j in range(16):
        out[j] = both


def product(parts):
    return pl.pallas_call(
        product_kernel,
        out_shape=jax.ShapeDtypeStruct((16, 12, parts.shape[2]), BF),
        in_specs=[WHOLE],
        out_specs=WHOLE,
        scratch_shapes=[pltpu.VMEM(parts.shape[1:], F32)],
        compiler_params=pltpu.CompilerParams(vmem_limit_bytes=8 * 2**20),
        cost_estimate=pl.CostEstimate(
            flops=parts.size, bytes_accessed=4 * parts.size, transcendentals=0
        ),
        name="product",
    )(parts)


def on_device(phi_occ, phi_vir, eps_occ, eps_vir, taus, pair_mask, basis):
    core, xh = lax.axis_index("core"), lax.axis_index("xh")
    naux, rows = basis.shape[1], phi_occ.shape[0]
    first = core == 0
    mask = jnp.pad(pair_mask.astype(BF), ((0, 0), (0, 120)))
    mine = jnp.concatenate(
        [phi_occ, phi_vir, basis, jnp.broadcast_to(mask, (rows, 128))], axis=1
    )
    up = from_tile(mine, 2)
    down = from_tile(mine, -4)
    mate = lax.ppermute(mine, "core", SWAP)
    moves = [(z * 16 + o, (o // 2) * 16 + z * 2 + o % 2) for z in range(8) for o in range(16)]
    part = lax.ppermute(basis, ("z", "xl", "y"), moves)
    got = trade(part, "y", 4)

    part_sums = green(
        core.reshape(1), taus, eps_occ[None], eps_vir[None], mine, mate, up, down
    )
    part_sums, part = lax.optimization_barrier((part_sums, part))
    sums = lax.all_to_all(part_sums, ORB, 0, 0, tiled=True)
    part = join(part, got, "y", 4, 0)
    got = trade(part, "y", 2)
    extra, x_mate, x_up, x_down = (slab[:, -naux - 128 :] for slab in (mine, mate, up, down))
    x_fourth = jnp.where(first, extra, x_down)

    def masks(slab):
        return slab[0, naux : naux + 8].astype(F32)

    m_own, m_mate, m_up, m_down = masks(extra), masks(x_mate), masks(x_up), masks(x_down)
    row_mask = jnp.stack(
        [m_own[5], m_own[0], jnp.where(first, m_mate[4], m_mate[6]), jnp.where(first, m_mate[3], m_mate[1])]
    )
    col_mask = jnp.stack(
        [m_up[2], m_down[7], jnp.where(first, m_up[3], m_up[1]), jnp.where(first, m_own[4], m_down[6])]
    )
    row_mask = jnp.repeat(row_mask, rows)
    col_mask = jnp.repeat(col_mask, rows)

    both = product(sums)
    both, part = lax.optimization_barrier((both, part))
    both = lax.all_to_all(both, ORB, 0, 0, tiled=True).reshape(2, rows, 4 * rows)
    part = join(part, got, "y", 2, 1)
    got = trade(part, "y", 1)
    by_row = (both.astype(F32) * row_mask).astype(BF)
    by_col = (both.astype(F32) * col_mask).astype(BF)

    def aux(slab):
        return slab[:, :naux]

    def rows_of(block, *panels):
        return jnp.einsum("trc,cq->trq", block, jnp.concatenate(panels), preferred_element_type=F32)

    def cols_of(block, panel):
        return jnp.einsum("trc,rq->tcq", block, panel, preferred_element_type=F32)

    r2, r3 = 2 * rows, 3 * rows
    to_up = cols_of(by_col[:, :, :rows], aux(extra)) + cols_of(by_col[:, :, r2:r3], aux(x_mate))
    last = cols_of(by_col[:, :, r3:], aux(x_mate))
    zero = jnp.zeros_like(last)
    to_down = cols_of(by_col[:, :, rows:r2], aux(extra)) + jnp.where(first, zero, last)
    to_mate = rows_of(by_row[:, :, r2:], aux(x_up), aux(x_fourth))
    own = rows_of(by_row[:, :, :r2], aux(x_up), aux(x_down)) + jnp.where(first, last, zero)
    to_up = to_up.astype(BF)
    got_up = from_tile(to_up, -2)
    got_down = from_tile(to_down.astype(BF), 4)
    got_mate = lax.ppermute(to_mate, "core", SWAP)
    projected = (own + got_mate + got_up.astype(F32) + got_down.astype(F32)).astype(BF)

    projected, part = lax.optimization_barrier((projected, part))
    gathered = to_all(projected, "z", 8)
    part = join(part, got, "y", 1, 0)
    part = join(part, trade(part, "xl", 1), "xl", 1, 1)
    blocks = part.reshape(2, 8, rows, naux)
    at = xh * 2 + core

    def response(flip):
        j = at ^ flip
        chosen = lax.dynamic_slice(
            blocks, (j // 2, 0, 0, (j % 2) * (naux // 2)), (1, 8, rows, naux // 2)
        )[0]
        return jnp.einsum("zrp,ztrq->ptq", chosen, gathered, preferred_element_type=F32)

    both_way = lax.ppermute(
        response(3).astype(BF), ("xh", "core"), [(0, 3), (3, 0), (1, 2), (2, 1)]
    )
    across = lax.ppermute(response(2).astype(BF), "xh", SWAP)
    beside = lax.ppermute(response(1), "core", SWAP)
    return response(0) + beside + across.astype(F32) + both_way.astype(F32)


def solution(mesh):
    names = ("z", "xh", "core", "xl", "y")
    fine = Mesh(mesh.devices.reshape(8, 2, 2, 2, 8), names)
    placed = (P(PTS, ORB), P(PTS, ORB), P(ORB), P(ORB), P(), P(PTS, None), P(PTS, ORB))

    return jax.shard_map(
        on_device, mesh=fine, in_specs=placed, out_specs=P(PTS, None, ORB), check_vma=False
    )
```

```python
import jax
import jax.numpy as jnp
from jax import lax
from jax.experimental import pallas as pl
from jax.experimental.pallas import tpu as pltpu
from jax.sharding import Mesh, PartitionSpec as P


ORB = ("xl", "y")
PTS = ("z", "xh", "core")
BF = jnp.bfloat16
F32 = jnp.float32
SWAP = [(0, 1), (1, 0)]
LAST = (((1,), (1,)), ((), ()))
FIRST = (((0,), (0,)), ((), ()))
WHOLE = pl.BlockSpec(memory_space=pltpu.VMEM)
SCALARS = pl.BlockSpec(memory_space=pltpu.SMEM)


def from_tile(value, steps):
    return lax.ppermute(value, PTS, [((i + steps) % 32, i) for i in range(32)])


def trade(value, axis, bit):
    size = lax.axis_size(axis)
    return lax.ppermute(value, axis, [(i, i ^ bit) for i in range(size)])


def join(value, got, axis, bit, at):
    upper = (lax.axis_index(axis) & bit) != 0
    return jnp.stack([jnp.where(upper, got, value), jnp.where(upper, value, got)], axis=at)


def green_kernel(core, taus, eps_occ, eps_vir, mine, mate, up, down, out, panel, left, total, rows12):
    rows = mine.shape[0]
    nocc, cols = eps_occ.shape[1], eps_occ.shape[1] + eps_vir.shape[1]
    panel[0:rows] = up[:, :cols]
    panel[rows : 2 * rows] = down[:, :cols]
    panel[2 * rows : 3 * rows] = up[:, :cols]

    @pl.when(core[0] == 0)
    def _():
        panel[3 * rows : 4 * rows] = mine[:, :cols]

    @pl.when(core[0] != 0)
    def _():
        panel[3 * rows : 4 * rows] = down[:, :cols]

    for t in range(2):
        for lo, hi, eps, sign in ((0, nocc, eps_occ, 1.0), (nocc, cols, eps_vir, -1.0)):
            expo = jnp.exp((sign * taus[t]) * eps[...])
            for s, slab in enumerate((mine, mate)):
                at = (2 * s + t) * rows
                left[at : at + rows, lo:hi] = (slab[:, lo:hi].astype(F32) * expo).astype(BF)
    lane = lax.broadcasted_iota(jnp.int32, (2 * rows, 4 * rows), 1)
    for q, (lo, hi) in enumerate(((0, nocc), (nocc, cols))):
        a = lax.dot_general(
            left[0 : 2 * rows, lo:hi], panel[:, lo:hi], LAST, preferred_element_type=F32
        )
        b = lax.dot_general(
            left[2 * rows : 4 * rows, lo:hi], panel[:, lo:hi], LAST, preferred_element_type=F32
        )
        total[q] = jnp.where(lane < 2 * rows, a, b)
    for j in range(16):
        rows12[j, 0:12] = total[0, 12 * j : 12 * j + 12]
        rows12[j, 12:24] = total[1, 12 * j : 12 * j + 12]
    out[...] = rows12[...].astype(BF)


def green(core, taus, eps_occ, eps_vir, mine, mate, up, down):
    rows, cols = mine.shape[0], eps_occ.shape[1] + eps_vir.shape[1]
    return pl.pallas_call(
        green_kernel,
        out_shape=jax.ShapeDtypeStruct((16, 24, 4 * rows), BF),
        in_specs=[SCALARS, SCALARS] + [WHOLE] * 6,
        out_specs=WHOLE,
        scratch_shapes=[
            pltpu.VMEM((4 * rows, cols), BF),
            pltpu.VMEM((4 * rows, cols), BF),
            pltpu.VMEM((2, 2 * rows, 4 * rows), F32),
            pltpu.VMEM((16, 24, 4 * rows), F32),
        ],
        compiler_params=pltpu.CompilerParams(vmem_limit_bytes=16 * 2**20),
        cost_estimate=pl.CostEstimate(
            flops=8 * rows * 4 * rows * cols, bytes_accessed=10 * rows * cols, transcendentals=4 * cols
        ),
        name="green",
    )(core, taus, eps_occ, eps_vir, mine, mate, up, down)


def product_kernel(parts, out, total):
    total[...] = parts[...].astype(F32).sum(axis=0)
    both = (total[0:12] * total[12:24]).astype(BF)
    for j in range(16):
        out[j] = both


def product(parts):
    return pl.pallas_call(
        product_kernel,
        out_shape=jax.ShapeDtypeStruct((16, 12, parts.shape[2]), BF),
        in_specs=[WHOLE],
        out_specs=WHOLE,
        scratch_shapes=[pltpu.VMEM(parts.shape[1:], F32)],
        compiler_params=pltpu.CompilerParams(vmem_limit_bytes=8 * 2**20),
        cost_estimate=pl.CostEstimate(
            flops=parts.size, bytes_accessed=4 * parts.size, transcendentals=0
        ),
        name="product",
    )(parts)


def project_kernel(core, parts, mine, mate, up, down, to_up, to_down, to_mate, own, chi, panel):
    rows, naux = own.shape[1], own.shape[2]
    lo = mine.shape[1] - naux - 128
    mid = lo + naux
    first = core[0] == 0
    for j in range(16):
        chi[12 * j : 12 * j + 12] = parts[j].astype(F32)
    lane = lax.broadcasted_iota(jnp.int32, (1, 128), 1)
    wide = lax.broadcasted_iota(jnp.int32, (1, 4 * rows), 1)
    weight = jnp.where(first, 1.0, 0.0).astype(F32)

    def pick(slab, slot):
        row = slab[0:8, mid : mid + 128].astype(F32)[0:1]
        return jnp.sum(jnp.where(lane == slot, row, 0.0), axis=1, keepdims=True)

    def spread(a, b, c, d):
        return jnp.where(
            wide < 2 * rows, jnp.where(wide < rows, a, b), jnp.where(wide < 3 * rows, c, d)
        )

    row_mask = spread(
        pick(mine, 5),
        pick(mine, 0),
        pick(mate, jnp.where(first, 4, 6)),
        pick(mate, jnp.where(first, 3, 1)),
    )
    col_mask = spread(
        pick(up, 2),
        pick(down, 7),
        pick(up, jnp.where(first, 3, 1)),
        pick(mine, 4) * weight + pick(down, 6) * (1.0 - weight),
    )
    panel[0:rows] = up[:, lo:mid]
    panel[rows : 2 * rows] = down[:, lo:mid]
    panel[2 * rows : 3 * rows] = up[:, lo:mid]

    @pl.when(first)
    def _():
        panel[3 * rows : 4 * rows] = mine[:, lo:mid]

    @pl.when(core[0] != 0)
    def _():
        panel[3 * rows : 4 * rows] = down[:, lo:mid]

    by_row = chi[...] * row_mask
    near = jnp.where(wide < 2 * rows, by_row, 0.0).astype(BF)
    far = jnp.where(wide < 2 * rows, 0.0, by_row).astype(BF)
    mine_rows = jnp.dot(near, panel[...], preferred_element_type=F32)
    mate_rows = jnp.dot(far, panel[...], preferred_element_type=F32)
    for t in range(2):
        by_col = (chi[t * rows : (t + 1) * rows] * col_mask).astype(BF)
        a = lax.dot_general(by_col, mine[:, lo:mid], FIRST, preferred_element_type=F32)
        b = lax.dot_general(by_col, mate[:, lo:mid], FIRST, preferred_element_type=F32)
        last = b[3 * rows :]
        to_up[t] = (a[:rows] + b[2 * rows : 3 * rows]).astype(BF)
        to_down[t] = (a[rows : 2 * rows] + last * (1.0 - weight)).astype(BF)
        own[t] = mine_rows[t * rows : (t + 1) * rows] + last * weight
        to_mate[t] = mate_rows[t * rows : (t + 1) * rows]


def project(core, parts, mine, mate, up, down, naux):
    rows = mine.shape[0]
    shape = (2, rows, naux)
    return pl.pallas_call(
        project_kernel,
        out_shape=(
            jax.ShapeDtypeStruct(shape, BF),
            jax.ShapeDtypeStruct(shape, BF),
            jax.ShapeDtypeStruct(shape, F32),
            jax.ShapeDtypeStruct(shape, F32),
        ),
        in_specs=[SCALARS] + [WHOLE] * 5,
        out_specs=(WHOLE,) * 4,
        scratch_shapes=[pltpu.VMEM((2 * rows, 4 * rows), F32), pltpu.VMEM((4 * rows, naux), BF)],
        compiler_params=pltpu.CompilerParams(vmem_limit_bytes=16 * 2**20),
        cost_estimate=pl.CostEstimate(
            flops=32 * rows * rows * naux, bytes_accessed=24 * rows * naux, transcendentals=0
        ),
        name="project",
    )(core, parts, mine, mate, up, down)


def combine_kernel(own, a, b, c, out):
    total = (own[...] + a[...] + b[...].astype(F32) + c[...].astype(F32)).astype(BF)
    for z in range(8):
        out[z] = total


def combine(own, a, b, c):
    return pl.pallas_call(
        combine_kernel,
        out_shape=jax.ShapeDtypeStruct((8,) + own.shape, BF),
        in_specs=[WHOLE] * 4,
        out_specs=WHOLE,
        compiler_params=pltpu.CompilerParams(vmem_limit_bytes=8 * 2**20),
        cost_estimate=pl.CostEstimate(
            flops=4 * own.size, bytes_accessed=28 * own.size, transcendentals=0
        ),
        name="combine",
    )(own, a, b, c)


def on_device(phi_occ, phi_vir, eps_occ, eps_vir, taus, pair_mask, basis):
    core, xh = lax.axis_index("core"), lax.axis_index("xh")
    naux, rows = basis.shape[1], phi_occ.shape[0]
    mask = jnp.pad(pair_mask.astype(BF), ((0, 0), (0, 120)))
    mine = jnp.concatenate(
        [phi_occ, phi_vir, basis, jnp.broadcast_to(mask, (rows, 128))], axis=1
    )
    up = from_tile(mine, 2)
    down = from_tile(mine, -4)
    mate = lax.ppermute(mine, "core", SWAP)
    got = []
    for m in range(4):
        pairs = [
            ((i // 2) * 16 + 2 * z + i % 2, z * 16 + (i ^ (2 * m)))
            for z in range(8)
            for i in range(16)
        ]
        got.append(lax.ppermute(basis, ("z", "xl", "y"), pairs))

    part_sums = green(
        core.reshape(1), taus, eps_occ[None], eps_vir[None], mine, mate, up, down
    )
    sums = lax.all_to_all(part_sums, ORB, 0, 0, tiled=True)
    y = lax.axis_index("y")
    odd, upper = (y & 2) != 0, (y & 4) != 0
    got = [jnp.where(odd, got[m ^ 1], got[m]) for m in range(4)]
    part = jnp.stack([jnp.where(upper, got[m ^ 2], got[m]) for m in range(4)])

    both = product(sums)
    both = lax.all_to_all(both, ORB, 0, 0, tiled=True)
    part = join(part, trade(part, "xl", 1), "xl", 1, 0)
    to_up, to_down, to_mate, own = project(core.reshape(1), both, mine, mate, up, down, naux)
    got_up = from_tile(to_up, -2)
    got_down = from_tile(to_down, 4)
    got_mate = lax.ppermute(to_mate, "core", SWAP)
    copies = combine(own, got_mate, got_up, got_down)
    gathered = lax.all_to_all(copies, "z", 0, 0, tiled=True)
    part = join(part, trade(part, "y", 1), "y", 1, 0)
    blocks = part.reshape(2, 8, rows, naux)
    at = xh * 2 + core

    def response(flip):
        j = at ^ flip
        chosen = lax.dynamic_slice(
            blocks, (j // 2, 0, 0, (j % 2) * (naux // 2)), (1, 8, rows, naux // 2)
        )[0]
        return jnp.einsum("zrp,ztrq->ptq", chosen, gathered, preferred_element_type=F32)

    both_way = lax.ppermute(
        response(3).astype(BF), ("xh", "core"), [(0, 3), (3, 0), (1, 2), (2, 1)]
    )
    across = lax.ppermute(response(2).astype(BF), "xh", SWAP)
    beside = lax.ppermute(response(1), "core", SWAP)
    return response(0) + beside + across.astype(F32) + both_way.astype(F32)


def solution(mesh):
    names = ("z", "xh", "core", "xl", "y")
    fine = Mesh(mesh.devices.reshape(8, 2, 2, 2, 8), names)
    placed = (P(PTS, ORB), P(PTS, ORB), P(ORB), P(ORB), P(), P(PTS, None), P(PTS, ORB))

    return jax.shard_map(
        on_device, mesh=fine, in_specs=placed, out_specs=P(PTS, None, ORB), check_vma=False
    )
```

```python
import jax
import jax.numpy as jnp
from jax import lax
from jax.experimental import pallas as pl
from jax.experimental.pallas import tpu as pltpu
from jax.sharding import Mesh, PartitionSpec as P


ORB = ("xl", "y")
PTS = ("z", "xh", "core")
BF = jnp.bfloat16
F32 = jnp.float32
SWAP = [(0, 1), (1, 0)]
LAST = (((1,), (1,)), ((), ()))
FIRST = (((0,), (0,)), ((), ()))
WHOLE = pl.BlockSpec(memory_space=pltpu.VMEM)
SCALARS = pl.BlockSpec(memory_space=pltpu.SMEM)


def from_tile(value, steps):
    return lax.ppermute(value, PTS, [((i + steps) % 32, i) for i in range(32)])


def trade(value, axis, bit):
    size = lax.axis_size(axis)
    return lax.ppermute(value, axis, [(i, i ^ bit) for i in range(size)])


def join(value, got, axis, bit, at):
    upper = (lax.axis_index(axis) & bit) != 0
    return jnp.stack([jnp.where(upper, got, value), jnp.where(upper, value, got)], axis=at)


def green_kernel(core, taus, eps_occ, eps_vir, mine, mate, up, down, out, panel, left, total, rows12):
    rows = mine.shape[0]
    nocc, cols = eps_occ.shape[1], eps_occ.shape[1] + eps_vir.shape[1]
    panel[0:rows] = up[:, :cols]
    panel[rows : 2 * rows] = down[:, :cols]
    panel[2 * rows : 3 * rows] = up[:, :cols]

    @pl.when(core[0] == 0)
    def _():
        panel[3 * rows : 4 * rows] = mine[:, :cols]

    @pl.when(core[0] != 0)
    def _():
        panel[3 * rows : 4 * rows] = down[:, :cols]

    for t in range(2):
        for lo, hi, eps, sign in ((0, nocc, eps_occ, 1.0), (nocc, cols, eps_vir, -1.0)):
            expo = jnp.exp((sign * taus[t]) * eps[...])
            for s, slab in enumerate((mine, mate)):
                at = (2 * s + t) * rows
                left[at : at + rows, lo:hi] = (slab[:, lo:hi].astype(F32) * expo).astype(BF)
    lane = lax.broadcasted_iota(jnp.int32, (2 * rows, 4 * rows), 1)
    for q, (lo, hi) in enumerate(((0, nocc), (nocc, cols))):
        a = lax.dot_general(
            left[0 : 2 * rows, lo:hi], panel[:, lo:hi], LAST, preferred_element_type=F32
        )
        b = lax.dot_general(
            left[2 * rows : 4 * rows, lo:hi], panel[:, lo:hi], LAST, preferred_element_type=F32
        )
        total[q] = jnp.where(lane < 2 * rows, a, b)
    for j in range(16):
        rows12[j, 0:12] = total[0, 12 * j : 12 * j + 12]
        rows12[j, 12:24] = total[1, 12 * j : 12 * j + 12]
    out[...] = rows12[...].astype(BF)


def green(core, taus, eps_occ, eps_vir, mine, mate, up, down):
    rows, cols = mine.shape[0], eps_occ.shape[1] + eps_vir.shape[1]
    return pl.pallas_call(
        green_kernel,
        out_shape=jax.ShapeDtypeStruct((16, 24, 4 * rows), BF),
        in_specs=[SCALARS, SCALARS] + [WHOLE] * 6,
        out_specs=WHOLE,
        scratch_shapes=[
            pltpu.VMEM((4 * rows, cols), BF),
            pltpu.VMEM((4 * rows, cols), BF),
            pltpu.VMEM((2, 2 * rows, 4 * rows), F32),
            pltpu.VMEM((16, 24, 4 * rows), F32),
        ],
        compiler_params=pltpu.CompilerParams(vmem_limit_bytes=16 * 2**20),
        cost_estimate=pl.CostEstimate(
            flops=8 * rows * 4 * rows * cols, bytes_accessed=10 * rows * cols, transcendentals=4 * cols
        ),
        name="green",
    )(core, taus, eps_occ, eps_vir, mine, mate, up, down)


def product_kernel(parts, out, total):
    total[...] = parts[...].astype(F32).sum(axis=0)
    both = (total[0:12] * total[12:24]).astype(BF)
    for j in range(16):
        out[j] = both


def product(parts):
    return pl.pallas_call(
        product_kernel,
        out_shape=jax.ShapeDtypeStruct((16, 12, parts.shape[2]), BF),
        in_specs=[WHOLE],
        out_specs=WHOLE,
        scratch_shapes=[pltpu.VMEM(parts.shape[1:], F32)],
        compiler_params=pltpu.CompilerParams(vmem_limit_bytes=8 * 2**20),
        cost_estimate=pl.CostEstimate(
            flops=parts.size, bytes_accessed=4 * parts.size, transcendentals=0
        ),
        name="product",
    )(parts)


def project_kernel(core, parts, mine, mate, up, down, to_up, to_down, to_mate, own, chi, panel):
    rows, naux = own.shape[1], own.shape[2]
    lo = mine.shape[1] - naux - 128
    mid = lo + naux
    first = core[0] == 0
    for j in range(16):
        chi[12 * j : 12 * j + 12] = parts[j].astype(F32)
    lane = lax.broadcasted_iota(jnp.int32, (1, 128), 1)
    wide = lax.broadcasted_iota(jnp.int32, (1, 4 * rows), 1)
    weight = jnp.where(first, 1.0, 0.0).astype(F32)

    def pick(slab, slot):
        row = slab[0:8, mid : mid + 128].astype(F32)[0:1]
        return jnp.sum(jnp.where(lane == slot, row, 0.0), axis=1, keepdims=True)

    def spread(a, b, c, d):
        return jnp.where(
            wide < 2 * rows, jnp.where(wide < rows, a, b), jnp.where(wide < 3 * rows, c, d)
        )

    row_mask = spread(
        pick(mine, 5),
        pick(mine, 0),
        pick(mate, jnp.where(first, 4, 6)),
        pick(mate, jnp.where(first, 3, 1)),
    )
    col_mask = spread(
        pick(up, 2),
        pick(down, 7),
        pick(up, jnp.where(first, 3, 1)),
        pick(mine, 4) * weight + pick(down, 6) * (1.0 - weight),
    )
    panel[0:rows] = up[:, lo:mid]
    panel[rows : 2 * rows] = down[:, lo:mid]
    panel[2 * rows : 3 * rows] = up[:, lo:mid]

    @pl.when(first)
    def _():
        panel[3 * rows : 4 * rows] = mine[:, lo:mid]

    @pl.when(core[0] != 0)
    def _():
        panel[3 * rows : 4 * rows] = down[:, lo:mid]

    by_row = chi[...] * row_mask
    near = jnp.where(wide < 2 * rows, by_row, 0.0).astype(BF)
    far = jnp.where(wide < 2 * rows, 0.0, by_row).astype(BF)
    mine_rows = jnp.dot(near, panel[...], preferred_element_type=F32)
    mate_rows = jnp.dot(far, panel[...], preferred_element_type=F32)
    for t in range(2):
        by_col = (chi[t * rows : (t + 1) * rows] * col_mask).astype(BF)
        a = lax.dot_general(by_col, mine[:, lo:mid], FIRST, preferred_element_type=F32)
        b = lax.dot_general(by_col, mate[:, lo:mid], FIRST, preferred_element_type=F32)
        last = b[3 * rows :]
        to_up[t] = (a[:rows] + b[2 * rows : 3 * rows]).astype(BF)
        to_down[t] = (a[rows : 2 * rows] + last * (1.0 - weight)).astype(BF)
        own[t] = mine_rows[t * rows : (t + 1) * rows] + last * weight
        to_mate[t] = mate_rows[t * rows : (t + 1) * rows]


def project(core, parts, mine, mate, up, down, naux):
    rows = mine.shape[0]
    shape = (2, rows, naux)
    return pl.pallas_call(
        project_kernel,
        out_shape=(
            jax.ShapeDtypeStruct(shape, BF),
            jax.ShapeDtypeStruct(shape, BF),
            jax.ShapeDtypeStruct(shape, F32),
            jax.ShapeDtypeStruct(shape, F32),
        ),
        in_specs=[SCALARS] + [WHOLE] * 5,
        out_specs=(WHOLE,) * 4,
        scratch_shapes=[pltpu.VMEM((2 * rows, 4 * rows), F32), pltpu.VMEM((4 * rows, naux), BF)],
        compiler_params=pltpu.CompilerParams(vmem_limit_bytes=16 * 2**20),
        cost_estimate=pl.CostEstimate(
            flops=32 * rows * rows * naux, bytes_accessed=24 * rows * naux, transcendentals=0
        ),
        name="project",
    )(core, parts, mine, mate, up, down)


def combine_kernel(own, a, b, c, out):
    total = (own[...] + a[...] + b[...].astype(F32) + c[...].astype(F32)).astype(BF)
    for z in range(8):
        out[z] = total


def combine(own, a, b, c):
    return pl.pallas_call(
        combine_kernel,
        out_shape=jax.ShapeDtypeStruct((8,) + own.shape, BF),
        in_specs=[WHOLE] * 4,
        out_specs=WHOLE,
        compiler_params=pltpu.CompilerParams(vmem_limit_bytes=8 * 2**20),
        cost_estimate=pl.CostEstimate(
            flops=4 * own.size, bytes_accessed=28 * own.size, transcendentals=0
        ),
        name="combine",
    )(own, a, b, c)


def on_device(phi_occ, phi_vir, eps_occ, eps_vir, taus, pair_mask, basis):
    core, xh = lax.axis_index("core"), lax.axis_index("xh")
    naux, rows = basis.shape[1], phi_occ.shape[0]
    got = []
    for far in (0, 4):
        pairs = [
            ((i // 2) * 16 + 2 * z + i % 2, z * 16 + (i ^ far)) for z in range(8) for i in range(16)
        ]
        got.append(lax.ppermute(basis, ("z", "xl", "y"), pairs))
    mask = jnp.pad(pair_mask.astype(BF), ((0, 0), (0, 120)))
    mine = jnp.concatenate(
        [phi_occ, phi_vir, basis, jnp.broadcast_to(mask, (rows, 128))], axis=1
    )
    up = from_tile(mine, 2)
    down = from_tile(mine, -4)
    mate = lax.ppermute(mine, "core", SWAP)
    part_sums = green(
        core.reshape(1), taus, eps_occ[None], eps_vir[None], mine, mate, up, down
    )
    sums = lax.all_to_all(part_sums, ORB, 0, 0, tiled=True)
    part = join(got[0], got[1], "y", 4, 0)
    got = trade(part, "y", 2)

    both = product(sums)
    both = lax.all_to_all(both, ORB, 0, 0, tiled=True)
    part = join(part, got, "y", 2, 1)
    part = join(part, trade(part, "xl", 1), "xl", 1, 0)
    to_up, to_down, to_mate, own = project(core.reshape(1), both, mine, mate, up, down, naux)
    got_up = from_tile(to_up, -2)
    got_down = from_tile(to_down, 4)
    got_mate = lax.ppermute(to_mate, "core", SWAP)
    copies = combine(own, got_mate, got_up, got_down)
    gathered = lax.all_to_all(copies, "z", 0, 0, tiled=True)
    part = join(part, trade(part, "y", 1), "y", 1, 0)
    blocks = part.reshape(2, 8, rows, naux)
    at = xh * 2 + core

    def response(flip):
        j = at ^ flip
        chosen = lax.dynamic_slice(
            blocks, (j // 2, 0, 0, (j % 2) * (naux // 2)), (1, 8, rows, naux // 2)
        )[0]
        return jnp.einsum("zrp,ztrq->ptq", chosen, gathered, preferred_element_type=F32)

    both_way = lax.ppermute(
        response(3).astype(BF), ("xh", "core"), [(0, 3), (3, 0), (1, 2), (2, 1)]
    )
    across = lax.ppermute(response(2).astype(BF), "xh", SWAP)
    beside = lax.ppermute(response(1), "core", SWAP)
    return response(0) + beside + across.astype(F32) + both_way.astype(F32)


def solution(mesh):
    names = ("z", "xh", "core", "xl", "y")
    fine = Mesh(mesh.devices.reshape(8, 2, 2, 2, 8), names)
    placed = (P(PTS, ORB), P(PTS, ORB), P(ORB), P(ORB), P(), P(PTS, None), P(PTS, ORB))

    return jax.shard_map(
        on_device, mesh=fine, in_specs=placed, out_specs=P(PTS, None, ORB), check_vma=False
    )
```

```python
import jax
import jax.numpy as jnp
from jax import lax
from jax.experimental import pallas as pl
from jax.experimental.pallas import tpu as pltpu
from jax.sharding import Mesh, PartitionSpec as P


ORB = ("xl", "y")
PTS = ("z", "xh", "core")
BF = jnp.bfloat16
F32 = jnp.float32
SWAP = [(0, 1), (1, 0)]
LAST = (((1,), (1,)), ((), ()))
FIRST = (((0,), (0,)), ((), ()))
WHOLE = pl.BlockSpec(memory_space=pltpu.VMEM)
SCALARS = pl.BlockSpec(memory_space=pltpu.SMEM)


def from_tile(value, steps):
    return lax.ppermute(value, PTS, [((i + steps) % 32, i) for i in range(32)])


def trade(value, axis, bit):
    size = lax.axis_size(axis)
    return lax.ppermute(value, axis, [(i, i ^ bit) for i in range(size)])


def join(value, got, axis, bit, at):
    upper = (lax.axis_index(axis) & bit) != 0
    return jnp.stack([jnp.where(upper, got, value), jnp.where(upper, value, got)], axis=at)


def green_kernel(core, expo_occ, expo_vir, mine, mate, up, down, out, panel, left, total, rows12):
    rows = mine.shape[0]
    nocc, cols = expo_occ.shape[1], expo_occ.shape[1] + expo_vir.shape[1]
    panel[0:rows] = up[:, :cols]
    panel[rows : 2 * rows] = down[:, :cols]
    panel[2 * rows : 3 * rows] = up[:, :cols]

    @pl.when(core[0] == 0)
    def _():
        panel[3 * rows : 4 * rows] = mine[:, :cols]

    @pl.when(core[0] != 0)
    def _():
        panel[3 * rows : 4 * rows] = down[:, :cols]

    for t in range(2):
        for lo, hi, expo in ((0, nocc, expo_occ), (nocc, cols, expo_vir)):
            for s, slab in enumerate((mine, mate)):
                at = (2 * s + t) * rows
                value = slab[:, lo:hi].astype(F32) * expo[t : t + 1]
                left[at : at + rows, lo:hi] = value.astype(BF)
    lane = lax.broadcasted_iota(jnp.int32, (2 * rows, 4 * rows), 1)
    for q, (lo, hi) in enumerate(((0, nocc), (nocc, cols))):
        a = lax.dot_general(
            left[0 : 2 * rows, lo:hi], panel[:, lo:hi], LAST, preferred_element_type=F32
        )
        b = lax.dot_general(
            left[2 * rows : 4 * rows, lo:hi], panel[:, lo:hi], LAST, preferred_element_type=F32
        )
        total[q] = jnp.where(lane < 2 * rows, a, b)
    for j in range(16):
        rows12[j, 0:12] = total[0, 12 * j : 12 * j + 12]
        rows12[j, 12:24] = total[1, 12 * j : 12 * j + 12]
    out[...] = rows12[...].astype(BF)


def green(core, expo_occ, expo_vir, mine, mate, up, down):
    rows, cols = mine.shape[0], expo_occ.shape[1] + expo_vir.shape[1]
    return pl.pallas_call(
        green_kernel,
        out_shape=jax.ShapeDtypeStruct((16, 24, 4 * rows), BF),
        in_specs=[SCALARS] + [WHOLE] * 6,
        out_specs=WHOLE,
        scratch_shapes=[
            pltpu.VMEM((4 * rows, cols), BF),
            pltpu.VMEM((4 * rows, cols), BF),
            pltpu.VMEM((2, 2 * rows, 4 * rows), F32),
            pltpu.VMEM((16, 24, 4 * rows), F32),
        ],
        compiler_params=pltpu.CompilerParams(vmem_limit_bytes=16 * 2**20),
        cost_estimate=pl.CostEstimate(
            flops=8 * rows * 4 * rows * cols, bytes_accessed=10 * rows * cols, transcendentals=0
        ),
        name="green",
    )(core, expo_occ, expo_vir, mine, mate, up, down)


def product_kernel(parts, out, total):
    total[...] = parts[...].astype(F32).sum(axis=0)
    both = (total[0:12] * total[12:24]).astype(BF)
    for j in range(16):
        out[j] = both


def product(parts):
    return pl.pallas_call(
        product_kernel,
        out_shape=jax.ShapeDtypeStruct((16, 12, parts.shape[2]), BF),
        in_specs=[WHOLE],
        out_specs=WHOLE,
        scratch_shapes=[pltpu.VMEM(parts.shape[1:], F32)],
        compiler_params=pltpu.CompilerParams(vmem_limit_bytes=8 * 2**20),
        cost_estimate=pl.CostEstimate(
            flops=parts.size, bytes_accessed=4 * parts.size, transcendentals=0
        ),
        name="product",
    )(parts)


def project_kernel(core, parts, mine, mate, up, down, to_up, to_down, to_mate, own, chi, panel):
    rows, naux = own.shape[1], own.shape[2]
    lo = mine.shape[1] - naux - 128
    mid = lo + naux
    first = core[0] == 0
    for j in range(16):
        chi[12 * j : 12 * j + 12] = parts[j].astype(F32)
    lane = lax.broadcasted_iota(jnp.int32, (1, 128), 1)
    wide = lax.broadcasted_iota(jnp.int32, (1, 4 * rows), 1)
    weight = jnp.where(first, 1.0, 0.0).astype(F32)

    def pick(slab, slot):
        row = slab[0:8, mid : mid + 128].astype(F32)[0:1]
        return jnp.sum(jnp.where(lane == slot, row, 0.0), axis=1, keepdims=True)

    def spread(a, b, c, d):
        return jnp.where(
            wide < 2 * rows, jnp.where(wide < rows, a, b), jnp.where(wide < 3 * rows, c, d)
        )

    row_mask = spread(
        pick(mine, 5),
        pick(mine, 0),
        pick(mate, jnp.where(first, 4, 6)),
        pick(mate, jnp.where(first, 3, 1)),
    )
    col_mask = spread(
        pick(up, 2),
        pick(down, 7),
        pick(up, jnp.where(first, 3, 1)),
        pick(mine, 4) * weight + pick(down, 6) * (1.0 - weight),
    )
    panel[0:rows] = up[:, lo:mid]
    panel[rows : 2 * rows] = down[:, lo:mid]
    panel[2 * rows : 3 * rows] = up[:, lo:mid]

    @pl.when(first)
    def _():
        panel[3 * rows : 4 * rows] = mine[:, lo:mid]

    @pl.when(core[0] != 0)
    def _():
        panel[3 * rows : 4 * rows] = down[:, lo:mid]

    by_row = chi[...] * row_mask
    near = jnp.where(wide < 2 * rows, by_row, 0.0).astype(BF)
    far = jnp.where(wide < 2 * rows, 0.0, by_row).astype(BF)
    mine_rows = jnp.dot(near, panel[...], preferred_element_type=F32)
    mate_rows = jnp.dot(far, panel[...], preferred_element_type=F32)
    for t in range(2):
        by_col = (chi[t * rows : (t + 1) * rows] * col_mask).astype(BF)
        a = lax.dot_general(by_col, mine[:, lo:mid], FIRST, preferred_element_type=F32)
        b = lax.dot_general(by_col, mate[:, lo:mid], FIRST, preferred_element_type=F32)
        last = b[3 * rows :]
        to_up[t] = (a[:rows] + b[2 * rows : 3 * rows]).astype(BF)
        to_down[t] = (a[rows : 2 * rows] + last * (1.0 - weight)).astype(BF)
        own[t] = mine_rows[t * rows : (t + 1) * rows] + last * weight
        to_mate[t] = mate_rows[t * rows : (t + 1) * rows]


def project(core, parts, mine, mate, up, down, naux):
    rows = mine.shape[0]
    shape = (2, rows, naux)
    return pl.pallas_call(
        project_kernel,
        out_shape=(
            jax.ShapeDtypeStruct(shape, BF),
            jax.ShapeDtypeStruct(shape, BF),
            jax.ShapeDtypeStruct(shape, F32),
            jax.ShapeDtypeStruct(shape, F32),
        ),
        in_specs=[SCALARS] + [WHOLE] * 5,
        out_specs=(WHOLE,) * 4,
        scratch_shapes=[pltpu.VMEM((2 * rows, 4 * rows), F32), pltpu.VMEM((4 * rows, naux), BF)],
        compiler_params=pltpu.CompilerParams(vmem_limit_bytes=16 * 2**20),
        cost_estimate=pl.CostEstimate(
            flops=32 * rows * rows * naux, bytes_accessed=24 * rows * naux, transcendentals=0
        ),
        name="project",
    )(core, parts, mine, mate, up, down)


def combine_kernel(own, a, b, c, out):
    total = (own[...] + a[...] + b[...].astype(F32) + c[...].astype(F32)).astype(BF)
    for z in range(8):
        out[z] = total


def combine(own, a, b, c):
    return pl.pallas_call(
        combine_kernel,
        out_shape=jax.ShapeDtypeStruct((8,) + own.shape, BF),
        in_specs=[WHOLE] * 4,
        out_specs=WHOLE,
        compiler_params=pltpu.CompilerParams(vmem_limit_bytes=8 * 2**20),
        cost_estimate=pl.CostEstimate(
            flops=4 * own.size, bytes_accessed=28 * own.size, transcendentals=0
        ),
        name="combine",
    )(own, a, b, c)


def on_device(phi_occ, phi_vir, eps_occ, eps_vir, taus, pair_mask, basis):
    core, xh = lax.axis_index("core"), lax.axis_index("xh")
    naux, rows = basis.shape[1], phi_occ.shape[0]
    mask = jnp.pad(pair_mask.astype(BF), ((0, 0), (0, 120)))
    mine = jnp.concatenate(
        [phi_occ, phi_vir, basis, jnp.broadcast_to(mask, (rows, 128))], axis=1
    )
    up = from_tile(mine, 2)
    down = from_tile(mine, -4)
    mate = lax.ppermute(mine, "core", SWAP)
    expo_occ = jnp.exp(taus[:, None] * eps_occ[None, :])
    expo_vir = jnp.exp(-taus[:, None] * eps_vir[None, :])
    part_sums = green(core.reshape(1), expo_occ, expo_vir, mine, mate, up, down)
    got = []
    for far in (0, 4):
        pairs = [
            ((i // 2) * 16 + 2 * z + i % 2, z * 16 + (i ^ far)) for z in range(8) for i in range(16)
        ]
        got.append(lax.ppermute(basis, ("z", "xl", "y"), pairs))
    sums = lax.all_to_all(part_sums, ORB, 0, 0, tiled=True)
    both = product(sums)
    both = lax.all_to_all(both, ORB, 0, 0, tiled=True)
    part = join(got[0], got[1], "y", 4, 0)
    part = join(part, trade(part, "y", 2), "y", 2, 1)
    part = join(part, trade(part, "xl", 1), "xl", 1, 0)
    to_up, to_down, to_mate, own = project(core.reshape(1), both, mine, mate, up, down, naux)
    got_up = from_tile(to_up, -2)
    got_down = from_tile(to_down, 4)
    got_mate = lax.ppermute(to_mate, "core", SWAP)
    copies = combine(own, got_mate, got_up, got_down)
    gathered = lax.all_to_all(copies, "z", 0, 0, tiled=True)
    part = join(part, trade(part, "y", 1), "y", 1, 0)
    blocks = part.reshape(2, 8, rows, naux)
    at = xh * 2 + core

    def response(flip):
        j = at ^ flip
        chosen = lax.dynamic_slice(
            blocks, (j // 2, 0, 0, (j % 2) * (naux // 2)), (1, 8, rows, naux // 2)
        )[0]
        return jnp.einsum("zrp,ztrq->ptq", chosen, gathered, preferred_element_type=F32)

    both_way = lax.ppermute(
        response(3).astype(BF), ("xh", "core"), [(0, 3), (3, 0), (1, 2), (2, 1)]
    )
    across = lax.ppermute(response(2).astype(BF), "xh", SWAP)
    beside = lax.ppermute(response(1), "core", SWAP)
    return response(0) + beside + across.astype(F32) + both_way.astype(F32)


def solution(mesh):
    names = ("z", "xh", "core", "xl", "y")
    fine = Mesh(mesh.devices.reshape(8, 2, 2, 2, 8), names)
    placed = (P(PTS, ORB), P(PTS, ORB), P(ORB), P(ORB), P(), P(PTS, None), P(PTS, ORB))

    return jax.shard_map(
        on_device, mesh=fine, in_specs=placed, out_specs=P(PTS, None, ORB), check_vma=False
    )
```

```python
import jax
import jax.numpy as jnp
from jax import lax
from jax.experimental import pallas as pl
from jax.experimental.pallas import tpu as pltpu
from jax.sharding import Mesh, PartitionSpec as P


ORB = ("xl", "y")
PTS = ("z", "xh", "core")
BF = jnp.bfloat16
F32 = jnp.float32
SWAP = [(0, 1), (1, 0)]
LAST = (((1,), (1,)), ((), ()))
FIRST = (((0,), (0,)), ((), ()))
WHOLE = pl.BlockSpec(memory_space=pltpu.VMEM)
SCALARS = pl.BlockSpec(memory_space=pltpu.SMEM)


def from_tile(value, steps):
    return lax.ppermute(value, PTS, [((i + steps) % 32, i) for i in range(32)])


def trade(value, axis, bit):
    size = lax.axis_size(axis)
    return lax.ppermute(value, axis, [(i, i ^ bit) for i in range(size)])


def join(value, got, axis, bit, at):
    upper = (lax.axis_index(axis) & bit) != 0
    return jnp.stack([jnp.where(upper, got, value), jnp.where(upper, value, got)], axis=at)


def green_kernel(core, expo_occ, expo_vir, mine, mate, up, down, out, panel, left, total, rows12):
    rows = mine.shape[0]
    nocc, cols = expo_occ.shape[1], expo_occ.shape[1] + expo_vir.shape[1]
    panel[0:rows] = up[:, :cols]
    panel[rows : 2 * rows] = down[:, :cols]
    panel[2 * rows : 3 * rows] = up[:, :cols]

    @pl.when(core[0] == 0)
    def _():
        panel[3 * rows : 4 * rows] = mine[:, :cols]

    @pl.when(core[0] != 0)
    def _():
        panel[3 * rows : 4 * rows] = down[:, :cols]

    for t in range(2):
        for lo, hi, expo in ((0, nocc, expo_occ), (nocc, cols, expo_vir)):
            for s, slab in enumerate((mine, mate)):
                at = (2 * s + t) * rows
                value = slab[:, lo:hi].astype(F32) * expo[t : t + 1]
                left[at : at + rows, lo:hi] = value.astype(BF)
    lane = lax.broadcasted_iota(jnp.int32, (2 * rows, 4 * rows), 1)
    for q, (lo, hi) in enumerate(((0, nocc), (nocc, cols))):
        a = lax.dot_general(
            left[0 : 2 * rows, lo:hi], panel[:, lo:hi], LAST, preferred_element_type=F32
        )
        b = lax.dot_general(
            left[2 * rows : 4 * rows, lo:hi], panel[:, lo:hi], LAST, preferred_element_type=F32
        )
        total[q] = jnp.where(lane < 2 * rows, a, b)
    for j in range(16):
        rows12[j, 0:12] = total[0, 12 * j : 12 * j + 12]
        rows12[j, 12:24] = total[1, 12 * j : 12 * j + 12]
    out[...] = rows12[...].astype(BF)


def green(core, expo_occ, expo_vir, mine, mate, up, down):
    rows, cols = mine.shape[0], expo_occ.shape[1] + expo_vir.shape[1]
    return pl.pallas_call(
        green_kernel,
        out_shape=jax.ShapeDtypeStruct((16, 24, 4 * rows), BF),
        in_specs=[SCALARS] + [WHOLE] * 6,
        out_specs=WHOLE,
        scratch_shapes=[
            pltpu.VMEM((4 * rows, cols), BF),
            pltpu.VMEM((4 * rows, cols), BF),
            pltpu.VMEM((2, 2 * rows, 4 * rows), F32),
            pltpu.VMEM((16, 24, 4 * rows), F32),
        ],
        compiler_params=pltpu.CompilerParams(vmem_limit_bytes=16 * 2**20),
        cost_estimate=pl.CostEstimate(
            flops=8 * rows * 4 * rows * cols, bytes_accessed=10 * rows * cols, transcendentals=0
        ),
        name="green",
    )(core, expo_occ, expo_vir, mine, mate, up, down)


def product_kernel(parts, out, total):
    total[...] = parts[...].astype(F32).sum(axis=0)
    both = (total[0:12] * total[12:24]).astype(BF)
    for j in range(16):
        out[j] = both


def product(parts):
    return pl.pallas_call(
        product_kernel,
        out_shape=jax.ShapeDtypeStruct((16, 12, parts.shape[2]), BF),
        in_specs=[WHOLE],
        out_specs=WHOLE,
        scratch_shapes=[pltpu.VMEM(parts.shape[1:], F32)],
        compiler_params=pltpu.CompilerParams(vmem_limit_bytes=8 * 2**20),
        cost_estimate=pl.CostEstimate(
            flops=parts.size, bytes_accessed=4 * parts.size, transcendentals=0
        ),
        name="product",
    )(parts)


def project_kernel(core, parts, mine, mate, up, down, to_up, to_down, to_mate, own, chi, panel):
    rows, naux = own.shape[1], own.shape[2]
    lo = mine.shape[1] - naux - 128
    mid = lo + naux
    first = core[0] == 0
    for j in range(16):
        chi[12 * j : 12 * j + 12] = parts[j].astype(F32)
    lane = lax.broadcasted_iota(jnp.int32, (1, 128), 1)
    wide = lax.broadcasted_iota(jnp.int32, (1, 4 * rows), 1)
    weight = jnp.where(first, 1.0, 0.0).astype(F32)

    def pick(slab, slot):
        row = slab[0:8, mid : mid + 128].astype(F32)[0:1]
        return jnp.sum(jnp.where(lane == slot, row, 0.0), axis=1, keepdims=True)

    def spread(a, b, c, d):
        return jnp.where(
            wide < 2 * rows, jnp.where(wide < rows, a, b), jnp.where(wide < 3 * rows, c, d)
        )

    row_mask = spread(
        pick(mine, 5),
        pick(mine, 0),
        pick(mate, jnp.where(first, 4, 6)),
        pick(mate, jnp.where(first, 3, 1)),
    )
    col_mask = spread(
        pick(up, 2),
        pick(down, 7),
        pick(up, jnp.where(first, 3, 1)),
        pick(mine, 4) * weight + pick(down, 6) * (1.0 - weight),
    )
    panel[0:rows] = up[:, lo:mid]
    panel[rows : 2 * rows] = down[:, lo:mid]
    panel[2 * rows : 3 * rows] = up[:, lo:mid]

    @pl.when(first)
    def _():
        panel[3 * rows : 4 * rows] = mine[:, lo:mid]

    @pl.when(core[0] != 0)
    def _():
        panel[3 * rows : 4 * rows] = down[:, lo:mid]

    by_row = chi[...] * row_mask
    near = jnp.where(wide < 2 * rows, by_row, 0.0).astype(BF)
    far = jnp.where(wide < 2 * rows, 0.0, by_row).astype(BF)
    mine_rows = jnp.dot(near, panel[...], preferred_element_type=F32)
    mate_rows = jnp.dot(far, panel[...], preferred_element_type=F32)
    for t in range(2):
        by_col = (chi[t * rows : (t + 1) * rows] * col_mask).astype(BF)
        a = lax.dot_general(by_col, mine[:, lo:mid], FIRST, preferred_element_type=F32)
        b = lax.dot_general(by_col, mate[:, lo:mid], FIRST, preferred_element_type=F32)
        last = b[3 * rows :]
        to_up[t] = (a[:rows] + b[2 * rows : 3 * rows]).astype(BF)
        to_down[t] = (a[rows : 2 * rows] + last * (1.0 - weight)).astype(BF)
        own[t] = mine_rows[t * rows : (t + 1) * rows] + last * weight
        to_mate[t] = mate_rows[t * rows : (t + 1) * rows]


def project(core, parts, mine, mate, up, down, naux):
    rows = mine.shape[0]
    shape = (2, rows, naux)
    return pl.pallas_call(
        project_kernel,
        out_shape=(
            jax.ShapeDtypeStruct(shape, BF),
            jax.ShapeDtypeStruct(shape, BF),
            jax.ShapeDtypeStruct(shape, F32),
            jax.ShapeDtypeStruct(shape, F32),
        ),
        in_specs=[SCALARS] + [WHOLE] * 5,
        out_specs=(WHOLE,) * 4,
        scratch_shapes=[pltpu.VMEM((2 * rows, 4 * rows), F32), pltpu.VMEM((4 * rows, naux), BF)],
        compiler_params=pltpu.CompilerParams(vmem_limit_bytes=16 * 2**20),
        cost_estimate=pl.CostEstimate(
            flops=32 * rows * rows * naux, bytes_accessed=24 * rows * naux, transcendentals=0
        ),
        name="project",
    )(core, parts, mine, mate, up, down)


def combine_kernel(own, a, b, c, out):
    total = (own[...] + a[...] + b[...].astype(F32) + c[...].astype(F32)).astype(BF)
    for z in range(8):
        out[z] = total


def combine(own, a, b, c):
    return pl.pallas_call(
        combine_kernel,
        out_shape=jax.ShapeDtypeStruct((8,) + own.shape, BF),
        in_specs=[WHOLE] * 4,
        out_specs=WHOLE,
        compiler_params=pltpu.CompilerParams(vmem_limit_bytes=8 * 2**20),
        cost_estimate=pl.CostEstimate(
            flops=4 * own.size, bytes_accessed=28 * own.size, transcendentals=0
        ),
        name="combine",
    )(own, a, b, c)


def finish_kernel(own, beside, across, diag, out):
    for t in range(2):
        out[:, t, :] = own[t] + beside[t] + across[t].astype(F32) + diag[t].astype(F32)


def finish(own, beside, across, diag):
    times, count, naux = own.shape
    return pl.pallas_call(
        finish_kernel,
        out_shape=jax.ShapeDtypeStruct((count, times, naux), F32),
        in_specs=[WHOLE] * 4,
        out_specs=WHOLE,
        compiler_params=pltpu.CompilerParams(vmem_limit_bytes=8 * 2**20),
        cost_estimate=pl.CostEstimate(
            flops=4 * own.size, bytes_accessed=16 * own.size, transcendentals=0
        ),
        name="finish",
    )(own, beside, across, diag)


def on_device(phi_occ, phi_vir, eps_occ, eps_vir, taus, pair_mask, basis):
    core, xh = lax.axis_index("core"), lax.axis_index("xh")
    naux, rows = basis.shape[1], phi_occ.shape[0]
    mask = jnp.pad(pair_mask.astype(BF), ((0, 0), (0, 120)))
    mine = jnp.concatenate(
        [phi_occ, phi_vir, basis, jnp.broadcast_to(mask, (rows, 128))], axis=1
    )
    up = from_tile(mine, 2)
    down = from_tile(mine, -4)
    mate = lax.ppermute(mine, "core", SWAP)
    expo_occ = jnp.exp(taus[:, None] * eps_occ[None, :])
    expo_vir = jnp.exp(-taus[:, None] * eps_vir[None, :])
    part_sums = green(core.reshape(1), expo_occ, expo_vir, mine, mate, up, down)
    got = []
    for far in (0, 4):
        pairs = [
            ((i // 2) * 16 + 2 * z + i % 2, z * 16 + (i ^ far)) for z in range(8) for i in range(16)
        ]
        got.append(lax.ppermute(basis, ("z", "xl", "y"), pairs))
    sums = lax.all_to_all(part_sums, ORB, 0, 0, tiled=True)
    both = product(sums)
    both = lax.all_to_all(both, ORB, 0, 0, tiled=True)
    to_up, to_down, to_mate, own = project(core.reshape(1), both, mine, mate, up, down, naux)
    got_up = from_tile(to_up, -2)
    got_down = from_tile(to_down, 4)
    got_mate = lax.ppermute(to_mate, "core", SWAP)
    copies = combine(own, got_mate, got_up, got_down)
    gathered = lax.all_to_all(copies, "z", 0, 0, tiled=True)
    part = join(got[0], got[1], "y", 4, 0)
    part = join(part, trade(part, "y", 2), "y", 2, 1)
    others = [part]
    for flip in (9, 8, 1):
        others.append(lax.ppermute(part, ORB, [(i, i ^ flip) for i in range(16)]))
    _, both, across_xl, across_y = others
    odd, right = (lax.axis_index("y") & 1) != 0, lax.axis_index("xl") != 0
    a = [jnp.where(odd, across_y, part), jnp.where(odd, part, across_y)]
    b = [jnp.where(odd, both, across_xl), jnp.where(odd, across_xl, both)]
    blocks = jnp.stack(
        [jnp.stack([jnp.where(right, b[h], a[h]), jnp.where(right, a[h], b[h])]) for h in range(2)]
    ).reshape(2, 8, rows, naux)
    at = xh * 2 + core

    def response(flip):
        j = at ^ flip
        chosen = lax.dynamic_slice(
            blocks, (j // 2, 0, 0, (j % 2) * (naux // 2)), (1, 8, rows, naux // 2)
        )[0]
        return jnp.einsum("zrp,ztrq->tpq", chosen, gathered, preferred_element_type=F32)

    both_way = lax.ppermute(
        response(3).astype(BF), ("xh", "core"), [(0, 3), (3, 0), (1, 2), (2, 1)]
    )
    across = lax.ppermute(response(2).astype(BF), "xh", SWAP)
    beside = lax.ppermute(response(1), "core", SWAP)
    return finish(response(0), beside, across, both_way)


def solution(mesh):
    names = ("z", "xh", "core", "xl", "y")
    fine = Mesh(mesh.devices.reshape(8, 2, 2, 2, 8), names)
    placed = (P(PTS, ORB), P(PTS, ORB), P(ORB), P(ORB), P(), P(PTS, None), P(PTS, ORB))

    return jax.shard_map(
        on_device, mesh=fine, in_specs=placed, out_specs=P(PTS, None, ORB), check_vma=False
    )
```

```python
import jax
import jax.numpy as jnp
from jax import lax
from jax.experimental import pallas as pl
from jax.experimental.pallas import tpu as pltpu
from jax.sharding import Mesh, PartitionSpec as P


ORB = ("xl", "y")
PTS = ("z", "xh", "core")
BF = jnp.bfloat16
F32 = jnp.float32
SWAP = [(0, 1), (1, 0)]
LAST = (((1,), (1,)), ((), ()))
FIRST = (((0,), (0,)), ((), ()))
WHOLE = pl.BlockSpec(memory_space=pltpu.VMEM)
SCALARS = pl.BlockSpec(memory_space=pltpu.SMEM)


def from_tile(value, steps):
    return lax.ppermute(value, PTS, [((i + steps) % 32, i) for i in range(32)])


def trade(value, axis, bit):
    size = lax.axis_size(axis)
    return lax.ppermute(value, axis, [(i, i ^ bit) for i in range(size)])


def join(value, got, axis, bit, at):
    upper = (lax.axis_index(axis) & bit) != 0
    return jnp.stack([jnp.where(upper, got, value), jnp.where(upper, value, got)], axis=at)


def green_kernel(core, expo_occ, expo_vir, mine, mate, up, down, out, panel, left, total, rows12):
    rows = mine.shape[0]
    nocc, cols = expo_occ.shape[1], expo_occ.shape[1] + expo_vir.shape[1]
    panel[0:rows] = up[:, :cols]
    panel[rows : 2 * rows] = down[:, :cols]
    panel[2 * rows : 3 * rows] = up[:, :cols]

    @pl.when(core[0] == 0)
    def _():
        panel[3 * rows : 4 * rows] = mine[:, :cols]

    @pl.when(core[0] != 0)
    def _():
        panel[3 * rows : 4 * rows] = down[:, :cols]

    for t in range(2):
        for lo, hi, expo in ((0, nocc, expo_occ), (nocc, cols, expo_vir)):
            for s, slab in enumerate((mine, mate)):
                at = (2 * s + t) * rows
                value = slab[:, lo:hi].astype(F32) * expo[t : t + 1]
                left[at : at + rows, lo:hi] = value.astype(BF)
    lane = lax.broadcasted_iota(jnp.int32, (2 * rows, 4 * rows), 1)
    for q, (lo, hi) in enumerate(((0, nocc), (nocc, cols))):
        a = lax.dot_general(
            left[0 : 2 * rows, lo:hi], panel[:, lo:hi], LAST, preferred_element_type=F32
        )
        b = lax.dot_general(
            left[2 * rows : 4 * rows, lo:hi], panel[:, lo:hi], LAST, preferred_element_type=F32
        )
        total[q] = jnp.where(lane < 2 * rows, a, b)
    for j in range(16):
        rows12[j, 0:12] = total[0, 12 * j : 12 * j + 12]
        rows12[j, 12:24] = total[1, 12 * j : 12 * j + 12]
    out[...] = rows12[...].astype(BF)


def green(core, expo_occ, expo_vir, mine, mate, up, down):
    rows, cols = mine.shape[0], expo_occ.shape[1] + expo_vir.shape[1]
    return pl.pallas_call(
        green_kernel,
        out_shape=jax.ShapeDtypeStruct((16, 24, 4 * rows), BF),
        in_specs=[SCALARS] + [WHOLE] * 6,
        out_specs=WHOLE,
        scratch_shapes=[
            pltpu.VMEM((4 * rows, cols), BF),
            pltpu.VMEM((4 * rows, cols), BF),
            pltpu.VMEM((2, 2 * rows, 4 * rows), F32),
            pltpu.VMEM((16, 24, 4 * rows), F32),
        ],
        compiler_params=pltpu.CompilerParams(vmem_limit_bytes=16 * 2**20),
        cost_estimate=pl.CostEstimate(
            flops=8 * rows * 4 * rows * cols, bytes_accessed=10 * rows * cols, transcendentals=0
        ),
        name="green",
    )(core, expo_occ, expo_vir, mine, mate, up, down)


def product_kernel(parts, out, total):
    total[...] = parts[...].astype(F32).sum(axis=0)
    both = (total[0:12] * total[12:24]).astype(BF)
    for j in range(16):
        out[j] = both


def product(parts):
    return pl.pallas_call(
        product_kernel,
        out_shape=jax.ShapeDtypeStruct((16, 12, parts.shape[2]), BF),
        in_specs=[WHOLE],
        out_specs=WHOLE,
        scratch_shapes=[pltpu.VMEM(parts.shape[1:], F32)],
        compiler_params=pltpu.CompilerParams(vmem_limit_bytes=8 * 2**20),
        cost_estimate=pl.CostEstimate(
            flops=parts.size, bytes_accessed=4 * parts.size, transcendentals=0
        ),
        name="product",
    )(parts)


def project_kernel(core, parts, mine, mate, up, down, to_up, to_down, to_mate, own, chi, panel):
    rows, naux = own.shape[1], own.shape[2]
    lo = mine.shape[1] - naux - 128
    mid = lo + naux
    first = core[0] == 0
    for j in range(16):
        chi[12 * j : 12 * j + 12] = parts[j].astype(F32)
    lane = lax.broadcasted_iota(jnp.int32, (1, 128), 1)
    wide = lax.broadcasted_iota(jnp.int32, (1, 4 * rows), 1)
    weight = jnp.where(first, 1.0, 0.0).astype(F32)

    def pick(slab, slot):
        row = slab[0:8, mid : mid + 128].astype(F32)[0:1]
        return jnp.sum(jnp.where(lane == slot, row, 0.0), axis=1, keepdims=True)

    def spread(a, b, c, d):
        return jnp.where(
            wide < 2 * rows, jnp.where(wide < rows, a, b), jnp.where(wide < 3 * rows, c, d)
        )

    row_mask = spread(
        pick(mine, 5),
        pick(mine, 0),
        pick(mate, jnp.where(first, 4, 6)),
        pick(mate, jnp.where(first, 3, 1)),
    )
    col_mask = spread(
        pick(up, 2),
        pick(down, 7),
        pick(up, jnp.where(first, 3, 1)),
        pick(mine, 4) * weight + pick(down, 6) * (1.0 - weight),
    )
    panel[0:rows] = up[:, lo:mid]
    panel[rows : 2 * rows] = down[:, lo:mid]
    panel[2 * rows : 3 * rows] = up[:, lo:mid]

    @pl.when(first)
    def _():
        panel[3 * rows : 4 * rows] = mine[:, lo:mid]

    @pl.when(core[0] != 0)
    def _():
        panel[3 * rows : 4 * rows] = down[:, lo:mid]

    by_row = chi[...] * row_mask
    near = jnp.where(wide < 2 * rows, by_row, 0.0).astype(BF)
    far = jnp.where(wide < 2 * rows, 0.0, by_row).astype(BF)
    mine_rows = jnp.dot(near, panel[...], preferred_element_type=F32)
    mate_rows = jnp.dot(far, panel[...], preferred_element_type=F32)
    for t in range(2):
        by_col = (chi[t * rows : (t + 1) * rows] * col_mask).astype(BF)
        a = lax.dot_general(by_col, mine[:, lo:mid], FIRST, preferred_element_type=F32)
        b = lax.dot_general(by_col, mate[:, lo:mid], FIRST, preferred_element_type=F32)
        last = b[3 * rows :]
        to_up[t] = (a[:rows] + b[2 * rows : 3 * rows]).astype(BF)
        to_down[t] = (a[rows : 2 * rows] + last * (1.0 - weight)).astype(BF)
        own[t] = mine_rows[t * rows : (t + 1) * rows] + last * weight
        to_mate[t] = mate_rows[t * rows : (t + 1) * rows]


def project(core, parts, mine, mate, up, down, naux):
    rows = mine.shape[0]
    shape = (2, rows, naux)
    return pl.pallas_call(
        project_kernel,
        out_shape=(
            jax.ShapeDtypeStruct(shape, BF),
            jax.ShapeDtypeStruct(shape, BF),
            jax.ShapeDtypeStruct(shape, F32),
            jax.ShapeDtypeStruct(shape, F32),
        ),
        in_specs=[SCALARS] + [WHOLE] * 5,
        out_specs=(WHOLE,) * 4,
        scratch_shapes=[pltpu.VMEM((2 * rows, 4 * rows), F32), pltpu.VMEM((4 * rows, naux), BF)],
        compiler_params=pltpu.CompilerParams(vmem_limit_bytes=16 * 2**20),
        cost_estimate=pl.CostEstimate(
            flops=32 * rows * rows * naux, bytes_accessed=24 * rows * naux, transcendentals=0
        ),
        name="project",
    )(core, parts, mine, mate, up, down)


def combine_kernel(own, a, b, c, out):
    total = (own[...] + a[...] + b[...].astype(F32) + c[...].astype(F32)).astype(BF)
    for z in range(8):
        out[z] = total


def combine(own, a, b, c):
    return pl.pallas_call(
        combine_kernel,
        out_shape=jax.ShapeDtypeStruct((8,) + own.shape, BF),
        in_specs=[WHOLE] * 4,
        out_specs=WHOLE,
        compiler_params=pltpu.CompilerParams(vmem_limit_bytes=8 * 2**20),
        cost_estimate=pl.CostEstimate(
            flops=4 * own.size, bytes_accessed=28 * own.size, transcendentals=0
        ),
        name="combine",
    )(own, a, b, c)


def finish_kernel(own, beside, across, diag, out):
    for t in range(2):
        out[:, t, :] = own[t] + beside[t] + across[t].astype(F32) + diag[t].astype(F32)


def finish(own, beside, across, diag):
    times, count, naux = own.shape
    return pl.pallas_call(
        finish_kernel,
        out_shape=jax.ShapeDtypeStruct((count, times, naux), F32),
        in_specs=[WHOLE] * 4,
        out_specs=WHOLE,
        compiler_params=pltpu.CompilerParams(vmem_limit_bytes=8 * 2**20),
        cost_estimate=pl.CostEstimate(
            flops=4 * own.size, bytes_accessed=16 * own.size, transcendentals=0
        ),
        name="finish",
    )(own, beside, across, diag)


def on_device(phi_occ, phi_vir, eps_occ, eps_vir, taus, pair_mask, basis):
    core, xh = lax.axis_index("core"), lax.axis_index("xh")
    naux, rows = basis.shape[1], phi_occ.shape[0]
    mask = jnp.broadcast_to(jnp.pad(pair_mask, ((0, 0), (0, 120))), (rows, 128))
    mine = jnp.concatenate([phi_occ, phi_vir, basis, mask.astype(BF)], axis=1)
    up = from_tile(mine, 2)
    down = from_tile(mine, -4)
    mate = lax.ppermute(mine, "core", SWAP)
    got = []
    for far in (0, 4):
        pairs = [
            ((i // 2) * 16 + 2 * z + i % 2, z * 16 + (i ^ far)) for z in range(8) for i in range(16)
        ]
        got.append(lax.ppermute(basis, ("z", "xl", "y"), pairs))
    expo_occ = jnp.exp(taus[:, None] * eps_occ[None, :])
    expo_vir = jnp.exp(-taus[:, None] * eps_vir[None, :])
    part_sums = green(core.reshape(1), expo_occ, expo_vir, mine, mate, up, down)
    sums = lax.all_to_all(part_sums, ORB, 0, 0, tiled=True)
    both = product(sums)
    both = lax.all_to_all(both, ORB, 0, 0, tiled=True)
    part = join(got[0], got[1], "y", 4, 0)
    part = join(part, trade(part, "y", 2), "y", 2, 1)
    to_up, to_down, to_mate, own = project(core.reshape(1), both, mine, mate, up, down, naux)
    got_up = from_tile(to_up, -2)
    got_down = from_tile(to_down, 4)
    got_mate = lax.ppermute(to_mate, "core", SWAP)
    copies = combine(own, got_mate, got_up, got_down)
    gathered = lax.all_to_all(copies, "z", 0, 0, tiled=True)
    others = [part]
    for flip in (9, 8, 1):
        others.append(lax.ppermute(part, ORB, [(i, i ^ flip) for i in range(16)]))
    _, both, across_xl, across_y = others
    odd, right = (lax.axis_index("y") & 1) != 0, lax.axis_index("xl") != 0
    a = [jnp.where(odd, across_y, part), jnp.where(odd, part, across_y)]
    b = [jnp.where(odd, both, across_xl), jnp.where(odd, across_xl, both)]
    blocks = jnp.stack(
        [jnp.stack([jnp.where(right, b[h], a[h]), jnp.where(right, a[h], b[h])]) for h in range(2)]
    ).reshape(2, 8, rows, naux)
    at = xh * 2 + core

    def response(flip):
        j = at ^ flip
        chosen = lax.dynamic_slice(
            blocks, (j // 2, 0, 0, (j % 2) * (naux // 2)), (1, 8, rows, naux // 2)
        )[0]
        return jnp.einsum("zrp,ztrq->tpq", chosen, gathered, preferred_element_type=F32)

    both_way = lax.ppermute(
        response(3).astype(BF), ("xh", "core"), [(0, 3), (3, 0), (1, 2), (2, 1)]
    )
    across = lax.ppermute(response(2).astype(BF), "xh", SWAP)
    beside = lax.ppermute(response(1), "core", SWAP)
    return finish(response(0), beside, across, both_way)


def solution(mesh):
    names = ("z", "xh", "core", "xl", "y")
    fine = Mesh(mesh.devices.reshape(8, 2, 2, 2, 8), names)
    placed = (P(PTS, ORB), P(PTS, ORB), P(ORB), P(ORB), P(), P(PTS, None), P(PTS, ORB))

    return jax.shard_map(
        on_device, mesh=fine, in_specs=placed, out_specs=P(PTS, None, ORB), check_vma=False
    )
```

```python
import jax
import jax.numpy as jnp
from jax import lax
from jax.experimental import pallas as pl
from jax.experimental.pallas import tpu as pltpu
from jax.sharding import Mesh, PartitionSpec as P


ORB = ("xl", "y")
PTS = ("z", "xh", "core")
BF = jnp.bfloat16
F32 = jnp.float32
SWAP = [(0, 1), (1, 0)]
LAST = (((1,), (1,)), ((), ()))
FIRST = (((0,), (0,)), ((), ()))
WHOLE = pl.BlockSpec(memory_space=pltpu.VMEM)
SCALARS = pl.BlockSpec(memory_space=pltpu.SMEM)


def from_tile(value, steps):
    return lax.ppermute(value, PTS, [((i + steps) % 32, i) for i in range(32)])


def trade(value, axis, bit):
    size = lax.axis_size(axis)
    return lax.ppermute(value, axis, [(i, i ^ bit) for i in range(size)])


def join(value, got, axis, bit, at):
    upper = (lax.axis_index(axis) & bit) != 0
    return jnp.stack([jnp.where(upper, got, value), jnp.where(upper, value, got)], axis=at)


def green_kernel(core, expo_occ, expo_vir, mine, mate, up, down, out, panel, left, total, rows12):
    rows = mine.shape[0]
    nocc, cols = expo_occ.shape[1], expo_occ.shape[1] + expo_vir.shape[1]
    panel[0:rows] = up[:, :cols]
    panel[rows : 2 * rows] = down[:, :cols]
    panel[2 * rows : 3 * rows] = up[:, :cols]

    @pl.when(core[0] == 0)
    def _():
        panel[3 * rows : 4 * rows] = mine[:, :cols]

    @pl.when(core[0] != 0)
    def _():
        panel[3 * rows : 4 * rows] = down[:, :cols]

    for t in range(2):
        for lo, hi, expo in ((0, nocc, expo_occ), (nocc, cols, expo_vir)):
            for s, slab in enumerate((mine, mate)):
                at = (2 * s + t) * rows
                value = slab[:, lo:hi].astype(F32) * expo[t : t + 1]
                left[at : at + rows, lo:hi] = value.astype(BF)
    lane = lax.broadcasted_iota(jnp.int32, (2 * rows, 4 * rows), 1)
    for q, (lo, hi) in enumerate(((0, nocc), (nocc, cols))):
        a = lax.dot_general(
            left[0 : 2 * rows, lo:hi], panel[:, lo:hi], LAST, preferred_element_type=F32
        )
        b = lax.dot_general(
            left[2 * rows : 4 * rows, lo:hi], panel[:, lo:hi], LAST, preferred_element_type=F32
        )
        total[q] = jnp.where(lane < 2 * rows, a, b)
    for j in range(16):
        rows12[j, 0:12] = total[0, 12 * j : 12 * j + 12]
        rows12[j, 12:24] = total[1, 12 * j : 12 * j + 12]
    out[...] = rows12[...].astype(BF)


def green(core, expo_occ, expo_vir, mine, mate, up, down):
    rows, cols = mine.shape[0], expo_occ.shape[1] + expo_vir.shape[1]
    return pl.pallas_call(
        green_kernel,
        out_shape=jax.ShapeDtypeStruct((16, 24, 4 * rows), BF),
        in_specs=[SCALARS] + [WHOLE] * 6,
        out_specs=WHOLE,
        scratch_shapes=[
            pltpu.VMEM((4 * rows, cols), BF),
            pltpu.VMEM((4 * rows, cols), BF),
            pltpu.VMEM((2, 2 * rows, 4 * rows), F32),
            pltpu.VMEM((16, 24, 4 * rows), F32),
        ],
        compiler_params=pltpu.CompilerParams(vmem_limit_bytes=16 * 2**20),
        cost_estimate=pl.CostEstimate(
            flops=8 * rows * 4 * rows * cols, bytes_accessed=10 * rows * cols, transcendentals=0
        ),
        name="green",
    )(core, expo_occ, expo_vir, mine, mate, up, down)


def product_kernel(parts, out, total):
    total[...] = parts[...].astype(F32).sum(axis=0)
    both = (total[0:12] * total[12:24]).astype(BF)
    for j in range(16):
        out[j] = both


def product(parts):
    return pl.pallas_call(
        product_kernel,
        out_shape=jax.ShapeDtypeStruct((16, 12, parts.shape[2]), BF),
        in_specs=[WHOLE],
        out_specs=WHOLE,
        scratch_shapes=[pltpu.VMEM(parts.shape[1:], F32)],
        compiler_params=pltpu.CompilerParams(vmem_limit_bytes=8 * 2**20),
        cost_estimate=pl.CostEstimate(
            flops=parts.size, bytes_accessed=4 * parts.size, transcendentals=0
        ),
        name="product",
    )(parts)


def project_kernel(core, parts, mine, mate, up, down, to_up, to_down, to_mate, own, chi, panel):
    rows, naux = own.shape[1], own.shape[2]
    lo = mine.shape[1] - naux - 128
    mid = lo + naux
    first = core[0] == 0
    for j in range(16):
        chi[12 * j : 12 * j + 12] = parts[j].astype(F32)
    lane = lax.broadcasted_iota(jnp.int32, (1, 128), 1)
    wide = lax.broadcasted_iota(jnp.int32, (1, 4 * rows), 1)
    weight = jnp.where(first, 1.0, 0.0).astype(F32)

    def pick(slab, slot):
        row = slab[0:8, mid : mid + 128].astype(F32)[0:1]
        return jnp.sum(jnp.where(lane == slot, row, 0.0), axis=1, keepdims=True)

    def spread(a, b, c, d):
        return jnp.where(
            wide < 2 * rows, jnp.where(wide < rows, a, b), jnp.where(wide < 3 * rows, c, d)
        )

    row_mask = spread(
        pick(mine, 5),
        pick(mine, 0),
        pick(mate, jnp.where(first, 4, 6)),
        pick(mate, jnp.where(first, 3, 1)),
    )
    col_mask = spread(
        pick(up, 2),
        pick(down, 7),
        pick(up, jnp.where(first, 3, 1)),
        pick(mine, 4) * weight + pick(down, 6) * (1.0 - weight),
    )
    panel[0:rows] = up[:, lo:mid]
    panel[rows : 2 * rows] = down[:, lo:mid]
    panel[2 * rows : 3 * rows] = up[:, lo:mid]

    @pl.when(first)
    def _():
        panel[3 * rows : 4 * rows] = mine[:, lo:mid]

    @pl.when(core[0] != 0)
    def _():
        panel[3 * rows : 4 * rows] = down[:, lo:mid]

    by_row = chi[...] * row_mask
    near = jnp.where(wide < 2 * rows, by_row, 0.0).astype(BF)
    far = jnp.where(wide < 2 * rows, 0.0, by_row).astype(BF)
    mine_rows = jnp.dot(near, panel[...], preferred_element_type=F32)
    mate_rows = jnp.dot(far, panel[...], preferred_element_type=F32)
    for t in range(2):
        by_col = (chi[t * rows : (t + 1) * rows] * col_mask).astype(BF)
        a = lax.dot_general(by_col, mine[:, lo:mid], FIRST, preferred_element_type=F32)
        b = lax.dot_general(by_col, mate[:, lo:mid], FIRST, preferred_element_type=F32)
        last = b[3 * rows :]
        to_up[t] = (a[:rows] + b[2 * rows : 3 * rows]).astype(BF)
        to_down[t] = (a[rows : 2 * rows] + last * (1.0 - weight)).astype(BF)
        own[t] = mine_rows[t * rows : (t + 1) * rows] + last * weight
        to_mate[t] = mate_rows[t * rows : (t + 1) * rows]


def project(core, parts, mine, mate, up, down, naux):
    rows = mine.shape[0]
    shape = (2, rows, naux)
    return pl.pallas_call(
        project_kernel,
        out_shape=(
            jax.ShapeDtypeStruct(shape, BF),
            jax.ShapeDtypeStruct(shape, BF),
            jax.ShapeDtypeStruct(shape, F32),
            jax.ShapeDtypeStruct(shape, F32),
        ),
        in_specs=[SCALARS] + [WHOLE] * 5,
        out_specs=(WHOLE,) * 4,
        scratch_shapes=[pltpu.VMEM((2 * rows, 4 * rows), F32), pltpu.VMEM((4 * rows, naux), BF)],
        compiler_params=pltpu.CompilerParams(vmem_limit_bytes=16 * 2**20),
        cost_estimate=pl.CostEstimate(
            flops=32 * rows * rows * naux, bytes_accessed=24 * rows * naux, transcendentals=0
        ),
        name="project",
    )(core, parts, mine, mate, up, down)


def combine_kernel(own, a, b, c, out):
    total = (own[...] + a[...] + b[...].astype(F32) + c[...].astype(F32)).astype(BF)
    for z in range(8):
        out[z] = total


def combine(own, a, b, c):
    return pl.pallas_call(
        combine_kernel,
        out_shape=jax.ShapeDtypeStruct((8,) + own.shape, BF),
        in_specs=[WHOLE] * 4,
        out_specs=WHOLE,
        compiler_params=pltpu.CompilerParams(vmem_limit_bytes=8 * 2**20),
        cost_estimate=pl.CostEstimate(
            flops=4 * own.size, bytes_accessed=28 * own.size, transcendentals=0
        ),
        name="combine",
    )(own, a, b, c)


def finish_kernel(own, beside, across, diag, out):
    for t in range(2):
        out[:, t, :] = own[t] + beside[t] + across[t].astype(F32) + diag[t].astype(F32)


def finish(own, beside, across, diag):
    times, count, naux = own.shape
    return pl.pallas_call(
        finish_kernel,
        out_shape=jax.ShapeDtypeStruct((count, times, naux), F32),
        in_specs=[WHOLE] * 4,
        out_specs=WHOLE,
        compiler_params=pltpu.CompilerParams(vmem_limit_bytes=8 * 2**20),
        cost_estimate=pl.CostEstimate(
            flops=4 * own.size, bytes_accessed=16 * own.size, transcendentals=0
        ),
        name="finish",
    )(own, beside, across, diag)


def on_device(phi_occ, phi_vir, eps_occ, eps_vir, taus, pair_mask, basis):
    core, xh = lax.axis_index("core"), lax.axis_index("xh")
    naux, rows = basis.shape[1], phi_occ.shape[0]
    mask = jnp.broadcast_to(jnp.pad(pair_mask, ((0, 0), (0, 120))), (rows, 128))
    mine = jnp.concatenate([phi_occ, phi_vir, basis, mask.astype(BF)], axis=1)
    up = from_tile(mine, 2)
    down = from_tile(mine, -4)
    mate = lax.ppermute(mine, "core", SWAP)
    pairs = [((i // 2) * 16 + 2 * z + i % 2, z * 16 + i) for z in range(8) for i in range(16)]
    part = lax.ppermute(basis, ("z", "xl", "y"), pairs)
    expo_occ = jnp.exp(taus[:, None] * eps_occ[None, :])
    expo_vir = jnp.exp(-taus[:, None] * eps_vir[None, :])
    part_sums = green(core.reshape(1), expo_occ, expo_vir, mine, mate, up, down)
    sums = lax.all_to_all(part_sums, ORB, 0, 0, tiled=True)
    both = product(sums)
    both = lax.all_to_all(both, ORB, 0, 0, tiled=True)
    part = join(part, trade(part, "y", 2), "y", 2, 0)
    part = join(part, trade(part, "y", 4), "y", 4, 0)
    to_up, to_down, to_mate, own = project(core.reshape(1), both, mine, mate, up, down, naux)
    got_up = from_tile(to_up, -2)
    got_down = from_tile(to_down, 4)
    got_mate = lax.ppermute(to_mate, "core", SWAP)
    copies = combine(own, got_mate, got_up, got_down)
    gathered = lax.all_to_all(copies, "z", 0, 0, tiled=True)
    others = [part]
    for flip in (9, 8, 1):
        others.append(lax.ppermute(part, ORB, [(i, i ^ flip) for i in range(16)]))
    _, both, across_xl, across_y = others
    odd, right = (lax.axis_index("y") & 1) != 0, lax.axis_index("xl") != 0
    a = [jnp.where(odd, across_y, part), jnp.where(odd, part, across_y)]
    b = [jnp.where(odd, both, across_xl), jnp.where(odd, across_xl, both)]
    blocks = jnp.stack(
        [jnp.stack([jnp.where(right, b[h], a[h]), jnp.where(right, a[h], b[h])]) for h in range(2)]
    ).reshape(2, 8, rows, naux)
    at = xh * 2 + core

    def response(flip):
        j = at ^ flip
        chosen = lax.dynamic_slice(
            blocks, (j // 2, 0, 0, (j % 2) * (naux // 2)), (1, 8, rows, naux // 2)
        )[0]
        return jnp.einsum("zrp,ztrq->tpq", chosen, gathered, preferred_element_type=F32)

    both_way = lax.ppermute(
        response(3).astype(BF), ("xh", "core"), [(0, 3), (3, 0), (1, 2), (2, 1)]
    )
    across = lax.ppermute(response(2).astype(BF), "xh", SWAP)
    beside = lax.ppermute(response(1), "core", SWAP)
    return finish(response(0), beside, across, both_way)


def solution(mesh):
    names = ("z", "xh", "core", "xl", "y")
    fine = Mesh(mesh.devices.reshape(8, 2, 2, 2, 8), names)
    placed = (P(PTS, ORB), P(PTS, ORB), P(ORB), P(ORB), P(), P(PTS, None), P(PTS, ORB))

    return jax.shard_map(
        on_device, mesh=fine, in_specs=placed, out_specs=P(PTS, None, ORB), check_vma=False
    )
```

```python
import jax
import jax.numpy as jnp
from jax import lax
from jax.experimental import pallas as pl
from jax.experimental.pallas import tpu as pltpu
from jax.sharding import Mesh, PartitionSpec as P


ORB = ("xl", "y")
PTS = ("z", "xh", "core")
BF = jnp.bfloat16
F32 = jnp.float32
SWAP = [(0, 1), (1, 0)]
LAST = (((1,), (1,)), ((), ()))
FIRST = (((0,), (0,)), ((), ()))
WHOLE = pl.BlockSpec(memory_space=pltpu.VMEM)
SCALARS = pl.BlockSpec(memory_space=pltpu.SMEM)


def from_tile(value, steps):
    return lax.ppermute(value, PTS, [((i + steps) % 32, i) for i in range(32)])


def trade(value, axis, bit):
    size = lax.axis_size(axis)
    return lax.ppermute(value, axis, [(i, i ^ bit) for i in range(size)])


def join(value, got, axis, bit, at):
    upper = (lax.axis_index(axis) & bit) != 0
    return jnp.stack([jnp.where(upper, got, value), jnp.where(upper, value, got)], axis=at)


def green_kernel(core, expo_occ, expo_vir, mine, mate, up, down, out, panel, left, total, rows12):
    rows = mine.shape[0]
    nocc, cols = expo_occ.shape[1], expo_occ.shape[1] + expo_vir.shape[1]
    panel[0:rows] = up[:, :cols]
    panel[rows : 2 * rows] = down[:, :cols]
    panel[2 * rows : 3 * rows] = up[:, :cols]

    @pl.when(core[0] == 0)
    def _():
        panel[3 * rows : 4 * rows] = mine[:, :cols]

    @pl.when(core[0] != 0)
    def _():
        panel[3 * rows : 4 * rows] = down[:, :cols]

    for t in range(2):
        for lo, hi, expo in ((0, nocc, expo_occ), (nocc, cols, expo_vir)):
            for s, slab in enumerate((mine, mate)):
                at = (2 * s + t) * rows
                value = slab[:, lo:hi].astype(F32) * expo[t : t + 1]
                left[at : at + rows, lo:hi] = value.astype(BF)
    lane = lax.broadcasted_iota(jnp.int32, (2 * rows, 4 * rows), 1)
    for q, (lo, hi) in enumerate(((0, nocc), (nocc, cols))):
        a = lax.dot_general(
            left[0 : 2 * rows, lo:hi], panel[:, lo:hi], LAST, preferred_element_type=F32
        )
        b = lax.dot_general(
            left[2 * rows : 4 * rows, lo:hi], panel[:, lo:hi], LAST, preferred_element_type=F32
        )
        total[q] = jnp.where(lane < 2 * rows, a, b)
    for j in range(16):
        rows12[j, 0:12] = total[0, 12 * j : 12 * j + 12]
        rows12[j, 12:24] = total[1, 12 * j : 12 * j + 12]
    out[...] = rows12[...].astype(BF)


def green(core, expo_occ, expo_vir, mine, mate, up, down):
    rows, cols = mine.shape[0], expo_occ.shape[1] + expo_vir.shape[1]
    return pl.pallas_call(
        green_kernel,
        out_shape=jax.ShapeDtypeStruct((16, 24, 4 * rows), BF),
        in_specs=[SCALARS] + [WHOLE] * 6,
        out_specs=WHOLE,
        scratch_shapes=[
            pltpu.VMEM((4 * rows, cols), BF),
            pltpu.VMEM((4 * rows, cols), BF),
            pltpu.VMEM((2, 2 * rows, 4 * rows), F32),
            pltpu.VMEM((16, 24, 4 * rows), F32),
        ],
        compiler_params=pltpu.CompilerParams(vmem_limit_bytes=16 * 2**20),
        cost_estimate=pl.CostEstimate(
            flops=8 * rows * 4 * rows * cols, bytes_accessed=10 * rows * cols, transcendentals=0
        ),
        name="green",
    )(core, expo_occ, expo_vir, mine, mate, up, down)


def product_kernel(parts, out, total):
    total[...] = parts[...].astype(F32).sum(axis=0)
    both = (total[0:12] * total[12:24]).astype(BF)
    for j in range(16):
        out[j] = both


def product(parts):
    return pl.pallas_call(
        product_kernel,
        out_shape=jax.ShapeDtypeStruct((16, 12, parts.shape[2]), BF),
        in_specs=[WHOLE],
        out_specs=WHOLE,
        scratch_shapes=[pltpu.VMEM(parts.shape[1:], F32)],
        compiler_params=pltpu.CompilerParams(vmem_limit_bytes=8 * 2**20),
        cost_estimate=pl.CostEstimate(
            flops=parts.size, bytes_accessed=4 * parts.size, transcendentals=0
        ),
        name="product",
    )(parts)


def project_kernel(core, parts, mine, mate, up, down, to_up, to_down, to_mate, own, chi, panel):
    rows, naux = own.shape[1], own.shape[2]
    lo = mine.shape[1] - naux - 128
    mid = lo + naux
    first = core[0] == 0
    for j in range(16):
        chi[12 * j : 12 * j + 12] = parts[j].astype(F32)
    lane = lax.broadcasted_iota(jnp.int32, (1, 128), 1)
    wide = lax.broadcasted_iota(jnp.int32, (1, 4 * rows), 1)
    weight = jnp.where(first, 1.0, 0.0).astype(F32)

    def pick(slab, slot):
        row = slab[0:8, mid : mid + 128].astype(F32)[0:1]
        return jnp.sum(jnp.where(lane == slot, row, 0.0), axis=1, keepdims=True)

    def spread(a, b, c, d):
        return jnp.where(
            wide < 2 * rows, jnp.where(wide < rows, a, b), jnp.where(wide < 3 * rows, c, d)
        )

    row_mask = spread(
        pick(mine, 5),
        pick(mine, 0),
        pick(mate, jnp.where(first, 4, 6)),
        pick(mate, jnp.where(first, 3, 1)),
    )
    col_mask = spread(
        pick(up, 2),
        pick(down, 7),
        pick(up, jnp.where(first, 3, 1)),
        pick(mine, 4) * weight + pick(down, 6) * (1.0 - weight),
    )
    panel[0:rows] = up[:, lo:mid]
    panel[rows : 2 * rows] = down[:, lo:mid]
    panel[2 * rows : 3 * rows] = up[:, lo:mid]

    @pl.when(first)
    def _():
        panel[3 * rows : 4 * rows] = mine[:, lo:mid]

    @pl.when(core[0] != 0)
    def _():
        panel[3 * rows : 4 * rows] = down[:, lo:mid]

    by_row = chi[...] * row_mask
    near = jnp.where(wide < 2 * rows, by_row, 0.0).astype(BF)
    far = jnp.where(wide < 2 * rows, 0.0, by_row).astype(BF)
    mine_rows = jnp.dot(near, panel[...], preferred_element_type=F32)
    mate_rows = jnp.dot(far, panel[...], preferred_element_type=F32)
    for t in range(2):
        by_col = (chi[t * rows : (t + 1) * rows] * col_mask).astype(BF)
        a = lax.dot_general(by_col, mine[:, lo:mid], FIRST, preferred_element_type=F32)
        b = lax.dot_general(by_col, mate[:, lo:mid], FIRST, preferred_element_type=F32)
        last = b[3 * rows :]
        to_up[t] = (a[:rows] + b[2 * rows : 3 * rows]).astype(BF)
        to_down[t] = (a[rows : 2 * rows] + last * (1.0 - weight)).astype(BF)
        own[t] = mine_rows[t * rows : (t + 1) * rows] + last * weight
        to_mate[t] = mate_rows[t * rows : (t + 1) * rows]


def project(core, parts, mine, mate, up, down, naux):
    rows = mine.shape[0]
    shape = (2, rows, naux)
    return pl.pallas_call(
        project_kernel,
        out_shape=(
            jax.ShapeDtypeStruct(shape, BF),
            jax.ShapeDtypeStruct(shape, BF),
            jax.ShapeDtypeStruct(shape, F32),
            jax.ShapeDtypeStruct(shape, F32),
        ),
        in_specs=[SCALARS] + [WHOLE] * 5,
        out_specs=(WHOLE,) * 4,
        scratch_shapes=[pltpu.VMEM((2 * rows, 4 * rows), F32), pltpu.VMEM((4 * rows, naux), BF)],
        compiler_params=pltpu.CompilerParams(vmem_limit_bytes=16 * 2**20),
        cost_estimate=pl.CostEstimate(
            flops=32 * rows * rows * naux, bytes_accessed=24 * rows * naux, transcendentals=0
        ),
        name="project",
    )(core, parts, mine, mate, up, down)


def combine_kernel(own, a, b, c, out):
    total = (own[...] + a[...] + b[...].astype(F32) + c[...].astype(F32)).astype(BF)
    for z in range(8):
        out[z] = total


def combine(own, a, b, c):
    return pl.pallas_call(
        combine_kernel,
        out_shape=jax.ShapeDtypeStruct((8,) + own.shape, BF),
        in_specs=[WHOLE] * 4,
        out_specs=WHOLE,
        compiler_params=pltpu.CompilerParams(vmem_limit_bytes=8 * 2**20),
        cost_estimate=pl.CostEstimate(
            flops=4 * own.size, bytes_accessed=28 * own.size, transcendentals=0
        ),
        name="combine",
    )(own, a, b, c)


def finish_kernel(x_hi, own, beside, across, out):
    for t in range(2):
        out[:, t, :] = own[t] + beside[x_hi[0], t] + across[t].astype(F32)


def finish(x_hi, own, beside, across):
    times, count, naux = own.shape
    return pl.pallas_call(
        finish_kernel,
        out_shape=jax.ShapeDtypeStruct((count, times, naux), F32),
        in_specs=[SCALARS] + [WHOLE] * 3,
        out_specs=WHOLE,
        compiler_params=pltpu.CompilerParams(vmem_limit_bytes=8 * 2**20),
        cost_estimate=pl.CostEstimate(
            flops=4 * own.size, bytes_accessed=16 * own.size, transcendentals=0
        ),
        name="finish",
    )(x_hi, own, beside, across)


def on_device(phi_occ, phi_vir, eps_occ, eps_vir, taus, pair_mask, basis):
    core, xh = lax.axis_index("core"), lax.axis_index("xh")
    naux, rows = basis.shape[1], phi_occ.shape[0]
    mask = jnp.broadcast_to(jnp.pad(pair_mask, ((0, 0), (0, 120))), (rows, 128))
    mine = jnp.concatenate([phi_occ, phi_vir, basis, mask.astype(BF)], axis=1)
    up = from_tile(mine, 2)
    down = from_tile(mine, -4)
    mate = lax.ppermute(mine, "core", SWAP)
    pairs = [((i // 2) * 16 + 2 * z + i % 2, z * 16 + i) for z in range(8) for i in range(16)]
    part = lax.ppermute(basis, ("z", "xl", "y"), pairs)
    expo_occ = jnp.exp(taus[:, None] * eps_occ[None, :])
    expo_vir = jnp.exp(-taus[:, None] * eps_vir[None, :])
    part_sums = green(core.reshape(1), expo_occ, expo_vir, mine, mate, up, down)
    sums = lax.all_to_all(part_sums, ORB, 0, 0, tiled=True)
    both = product(sums)
    both = lax.all_to_all(both, ORB, 0, 0, tiled=True)
    part = join(part, trade(part, "y", 2), "y", 2, 0)
    part = join(part, trade(part, "y", 4), "y", 4, 0)
    to_up, to_down, to_mate, own = project(core.reshape(1), both, mine, mate, up, down, naux)
    got_up = from_tile(to_up, -2)
    got_down = from_tile(to_down, 4)
    got_mate = lax.ppermute(to_mate, "core", SWAP)
    copies = combine(own, got_mate, got_up, got_down)
    gathered = lax.all_to_all(copies, "z", 0, 0, tiled=True)
    others = [part]
    for flip in (9, 8, 1):
        others.append(lax.ppermute(part, ORB, [(i, i ^ flip) for i in range(16)]))
    _, both, across_xl, across_y = others
    odd, right = (lax.axis_index("y") & 1) != 0, lax.axis_index("xl") != 0
    a = [jnp.where(odd, across_y, part), jnp.where(odd, part, across_y)]
    b = [jnp.where(odd, both, across_xl), jnp.where(odd, across_xl, both)]
    blocks = jnp.stack(
        [jnp.stack([jnp.where(right, b[h], a[h]), jnp.where(right, a[h], b[h])]) for h in range(2)]
    ).reshape(2, 8, rows, naux)

    def chosen(half, part_of):
        start = (half, 0, 0, part_of * (naux // 2))
        return lax.dynamic_slice(blocks, start, (1, 8, rows, naux // 2))[0]

    def response(cols):
        return jnp.einsum("zrp,ztrq->tpq", cols, gathered, preferred_element_type=F32)

    start = (0, 0, 0, (1 - core) * (naux // 2))
    others = lax.dynamic_slice(blocks, start, (2, 8, rows, naux // 2))
    pair = jnp.einsum("hzrp,ztrq->htpq", others, gathered, preferred_element_type=F32)
    beside = lax.ppermute(pair, "core", SWAP)
    mine_here, mine_there = response(chosen(xh, core)), response(chosen(1 - xh, core))
    there = lax.dynamic_index_in_dim(beside, 1 - xh, 0, keepdims=False)
    across = lax.ppermute((mine_there + there).astype(BF), "xh", SWAP)
    return finish(xh.reshape(1), mine_here, beside, across)


def solution(mesh):
    names = ("z", "xh", "core", "xl", "y")
    fine = Mesh(mesh.devices.reshape(8, 2, 2, 2, 8), names)
    placed = (P(PTS, ORB), P(PTS, ORB), P(ORB), P(ORB), P(), P(PTS, None), P(PTS, ORB))

    return jax.shard_map(
        on_device, mesh=fine, in_specs=placed, out_specs=P(PTS, None, ORB), check_vma=False
    )
```

```python
import jax
import jax.numpy as jnp
from jax import lax
from jax.experimental import pallas as pl
from jax.experimental.pallas import tpu as pltpu
from jax.sharding import Mesh, PartitionSpec as P


ORB = ("xl", "y")
PTS = ("z", "xh", "core")
BF = jnp.bfloat16
F32 = jnp.float32
SWAP = [(0, 1), (1, 0)]
LAST = (((1,), (1,)), ((), ()))
FIRST = (((0,), (0,)), ((), ()))
WHOLE = pl.BlockSpec(memory_space=pltpu.VMEM)
SCALARS = pl.BlockSpec(memory_space=pltpu.SMEM)


def from_tile(value, steps):
    return lax.ppermute(value, PTS, [((i + steps) % 32, i) for i in range(32)])


def trade(value, axis, bit):
    size = lax.axis_size(axis)
    return lax.ppermute(value, axis, [(i, i ^ bit) for i in range(size)])


def join(value, got, axis, bit, at):
    upper = (lax.axis_index(axis) & bit) != 0
    return jnp.stack([jnp.where(upper, got, value), jnp.where(upper, value, got)], axis=at)


def green_kernel(core, expo_occ, expo_vir, mine, mate, up, down, out, panel, left, total, rows12):
    rows = mine.shape[0]
    nocc, cols = expo_occ.shape[1], expo_occ.shape[1] + expo_vir.shape[1]
    panel[0:rows] = up[:, :cols]
    panel[rows : 2 * rows] = down[:, :cols]
    panel[2 * rows : 3 * rows] = up[:, :cols]

    @pl.when(core[0] == 0)
    def _():
        panel[3 * rows : 4 * rows] = mine[:, :cols]

    @pl.when(core[0] != 0)
    def _():
        panel[3 * rows : 4 * rows] = down[:, :cols]

    for t in range(2):
        for lo, hi, expo in ((0, nocc, expo_occ), (nocc, cols, expo_vir)):
            for s, slab in enumerate((mine, mate)):
                at = (2 * s + t) * rows
                value = slab[:, lo:hi].astype(F32) * expo[t : t + 1]
                left[at : at + rows, lo:hi] = value.astype(BF)
    for q, (lo, hi) in enumerate(((0, nocc), (nocc, cols))):
        for s in range(2):
            at = 2 * s * rows
            total[q, :, at : at + 2 * rows] = lax.dot_general(
                left[at : at + 2 * rows, lo:hi],
                panel[at : at + 2 * rows, lo:hi],
                LAST,
                preferred_element_type=F32,
            )
    for j in range(16):
        rows12[j, 0:12] = total[0, 12 * j : 12 * j + 12]
        rows12[j, 12:24] = total[1, 12 * j : 12 * j + 12]
    out[...] = rows12[...].astype(BF)


def green(core, expo_occ, expo_vir, mine, mate, up, down):
    rows, cols = mine.shape[0], expo_occ.shape[1] + expo_vir.shape[1]
    return pl.pallas_call(
        green_kernel,
        out_shape=jax.ShapeDtypeStruct((16, 24, 4 * rows), BF),
        in_specs=[SCALARS] + [WHOLE] * 6,
        out_specs=WHOLE,
        scratch_shapes=[
            pltpu.VMEM((4 * rows, cols), BF),
            pltpu.VMEM((4 * rows, cols), BF),
            pltpu.VMEM((2, 2 * rows, 4 * rows), F32),
            pltpu.VMEM((16, 24, 4 * rows), F32),
        ],
        compiler_params=pltpu.CompilerParams(vmem_limit_bytes=16 * 2**20),
        cost_estimate=pl.CostEstimate(
            flops=8 * rows * 4 * rows * cols, bytes_accessed=10 * rows * cols, transcendentals=0
        ),
        name="green",
    )(core, expo_occ, expo_vir, mine, mate, up, down)


def product_kernel(parts, out, total):
    total[...] = parts[...].astype(F32).sum(axis=0)
    both = (total[0:12] * total[12:24]).astype(BF)
    for j in range(16):
        out[j] = both


def product(parts):
    return pl.pallas_call(
        product_kernel,
        out_shape=jax.ShapeDtypeStruct((16, 12, parts.shape[2]), BF),
        in_specs=[WHOLE],
        out_specs=WHOLE,
        scratch_shapes=[pltpu.VMEM(parts.shape[1:], F32)],
        compiler_params=pltpu.CompilerParams(vmem_limit_bytes=8 * 2**20),
        cost_estimate=pl.CostEstimate(
            flops=parts.size, bytes_accessed=4 * parts.size, transcendentals=0
        ),
        name="product",
    )(parts)


def project_kernel(core, parts, mine, mate, up, down, to_up, to_down, to_mate, own, chi, panel):
    rows, naux = own.shape[1], own.shape[2]
    lo = mine.shape[1] - naux - 128
    mid = lo + naux
    first = core[0] == 0
    for j in range(16):
        chi[12 * j : 12 * j + 12] = parts[j].astype(F32)
    lane = lax.broadcasted_iota(jnp.int32, (1, 128), 1)
    wide = lax.broadcasted_iota(jnp.int32, (1, 4 * rows), 1)
    weight = jnp.where(first, 1.0, 0.0).astype(F32)

    def pick(slab, slot):
        row = slab[0:8, mid : mid + 128].astype(F32)[0:1]
        return jnp.sum(jnp.where(lane == slot, row, 0.0), axis=1, keepdims=True)

    def spread(a, b, c, d):
        return jnp.where(
            wide < 2 * rows, jnp.where(wide < rows, a, b), jnp.where(wide < 3 * rows, c, d)
        )

    row_mask = spread(
        pick(mine, 5),
        pick(mine, 0),
        pick(mate, jnp.where(first, 4, 6)),
        pick(mate, jnp.where(first, 3, 1)),
    )
    col_mask = spread(
        pick(up, 2),
        pick(down, 7),
        pick(up, jnp.where(first, 3, 1)),
        pick(mine, 4) * weight + pick(down, 6) * (1.0 - weight),
    )
    panel[0:rows] = up[:, lo:mid]
    panel[rows : 2 * rows] = down[:, lo:mid]
    panel[2 * rows : 3 * rows] = up[:, lo:mid]

    @pl.when(first)
    def _():
        panel[3 * rows : 4 * rows] = mine[:, lo:mid]

    @pl.when(core[0] != 0)
    def _():
        panel[3 * rows : 4 * rows] = down[:, lo:mid]

    by_row = chi[...] * row_mask
    near = jnp.where(wide < 2 * rows, by_row, 0.0).astype(BF)
    far = jnp.where(wide < 2 * rows, 0.0, by_row).astype(BF)
    mine_rows = jnp.dot(near, panel[...], preferred_element_type=F32)
    mate_rows = jnp.dot(far, panel[...], preferred_element_type=F32)
    for t in range(2):
        by_col = (chi[t * rows : (t + 1) * rows] * col_mask).astype(BF)
        a = lax.dot_general(by_col, mine[:, lo:mid], FIRST, preferred_element_type=F32)
        b = lax.dot_general(by_col, mate[:, lo:mid], FIRST, preferred_element_type=F32)
        last = b[3 * rows :]
        to_up[t] = (a[:rows] + b[2 * rows : 3 * rows]).astype(BF)
        to_down[t] = (a[rows : 2 * rows] + last * (1.0 - weight)).astype(BF)
        own[t] = mine_rows[t * rows : (t + 1) * rows] + last * weight
        to_mate[t] = mate_rows[t * rows : (t + 1) * rows]


def project(core, parts, mine, mate, up, down, naux):
    rows = mine.shape[0]
    shape = (2, rows, naux)
    return pl.pallas_call(
        project_kernel,
        out_shape=(
            jax.ShapeDtypeStruct(shape, BF),
            jax.ShapeDtypeStruct(shape, BF),
            jax.ShapeDtypeStruct(shape, F32),
            jax.ShapeDtypeStruct(shape, F32),
        ),
        in_specs=[SCALARS] + [WHOLE] * 5,
        out_specs=(WHOLE,) * 4,
        scratch_shapes=[pltpu.VMEM((2 * rows, 4 * rows), F32), pltpu.VMEM((4 * rows, naux), BF)],
        compiler_params=pltpu.CompilerParams(vmem_limit_bytes=16 * 2**20),
        cost_estimate=pl.CostEstimate(
            flops=32 * rows * rows * naux, bytes_accessed=24 * rows * naux, transcendentals=0
        ),
        name="project",
    )(core, parts, mine, mate, up, down)


def combine_kernel(own, a, b, c, out):
    total = (own[...] + a[...] + b[...].astype(F32) + c[...].astype(F32)).astype(BF)
    for z in range(8):
        out[z] = total


def combine(own, a, b, c):
    return pl.pallas_call(
        combine_kernel,
        out_shape=jax.ShapeDtypeStruct((8,) + own.shape, BF),
        in_specs=[WHOLE] * 4,
        out_specs=WHOLE,
        compiler_params=pltpu.CompilerParams(vmem_limit_bytes=8 * 2**20),
        cost_estimate=pl.CostEstimate(
            flops=4 * own.size, bytes_accessed=28 * own.size, transcendentals=0
        ),
        name="combine",
    )(own, a, b, c)


def finish_kernel(own, here, across, out):
    for t in range(2):
        out[:, t, :] = own[t] + here[t] + across[t].astype(F32)


def finish(own, here, across):
    times, count, naux = own.shape
    return pl.pallas_call(
        finish_kernel,
        out_shape=jax.ShapeDtypeStruct((count, times, naux), F32),
        in_specs=[WHOLE] * 3,
        out_specs=WHOLE,
        compiler_params=pltpu.CompilerParams(vmem_limit_bytes=8 * 2**20),
        cost_estimate=pl.CostEstimate(
            flops=4 * own.size, bytes_accessed=16 * own.size, transcendentals=0
        ),
        name="finish",
    )(own, here, across)


def on_device(phi_occ, phi_vir, eps_occ, eps_vir, taus, pair_mask, basis):
    core, xh = lax.axis_index("core"), lax.axis_index("xh")
    naux, rows = basis.shape[1], phi_occ.shape[0]
    mask = jnp.broadcast_to(jnp.pad(pair_mask, ((0, 0), (0, 120))), (rows, 128))
    mine = jnp.concatenate([phi_occ, phi_vir, basis, mask.astype(BF)], axis=1)
    up = from_tile(mine, 2)
    down = from_tile(mine, -4)
    mate = lax.ppermute(mine, "core", SWAP)
    pairs = [((i // 2) * 16 + 2 * z + i % 2, z * 16 + i) for z in range(8) for i in range(16)]
    part = lax.ppermute(basis, ("z", "xl", "y"), pairs)
    expo_occ = jnp.exp(taus[:, None] * eps_occ[None, :])
    expo_vir = jnp.exp(-taus[:, None] * eps_vir[None, :])
    part_sums = green(core.reshape(1), expo_occ, expo_vir, mine, mate, up, down)
    sums = lax.all_to_all(part_sums, ORB, 0, 0, tiled=True)
    both = product(sums)
    both = lax.all_to_all(both, ORB, 0, 0, tiled=True)
    got = trade(part, "y", 2)
    to_up, to_down, to_mate, own = project(core.reshape(1), both, mine, mate, up, down, naux)
    got_up = from_tile(to_up, -2)
    got_down = from_tile(to_down, 4)
    got_mate = lax.ppermute(to_mate, "core", SWAP)
    copies = combine(own, got_mate, got_up, got_down)
    gathered = lax.all_to_all(copies, "z", 0, 0, tiled=True)
    part = join(part, got, "y", 2, 0)
    part = join(part, trade(part, "y", 4), "y", 4, 0)
    others = [part]
    for flip in (9, 8, 1):
        others.append(lax.ppermute(part, ORB, [(i, i ^ flip) for i in range(16)]))
    _, both, across_xl, across_y = others
    odd, right = (lax.axis_index("y") & 1) != 0, lax.axis_index("xl") != 0
    a = [jnp.where(odd, across_y, part), jnp.where(odd, part, across_y)]
    b = [jnp.where(odd, both, across_xl), jnp.where(odd, across_xl, both)]
    blocks = jnp.stack(
        [jnp.stack([jnp.where(right, b[h], a[h]), jnp.where(right, a[h], b[h])]) for h in range(2)]
    ).reshape(2, 8, rows, naux)

    def chosen(half, part_of):
        start = (half, 0, 0, part_of * (naux // 2))
        return lax.dynamic_slice(blocks, start, (1, 8, rows, naux // 2))[0]

    def response(cols):
        return jnp.einsum("zrp,ztrq->tpq", cols, gathered, preferred_element_type=F32)

    there = lax.ppermute(response(chosen(1 - xh, 1 - core)).astype(BF), "core", SWAP)
    total = response(chosen(1 - xh, core)) + there.astype(F32)
    across = lax.ppermute(total.astype(BF), "xh", SWAP)
    here = lax.ppermute(response(chosen(xh, 1 - core)), "core", SWAP)
    own = response(chosen(xh, core))
    return finish(own, here, across)


def solution(mesh):
    names = ("z", "xh", "core", "xl", "y")
    fine = Mesh(mesh.devices.reshape(8, 2, 2, 2, 8), names)
    placed = (P(PTS, ORB), P(PTS, ORB), P(ORB), P(ORB), P(), P(PTS, None), P(PTS, ORB))

    return jax.shard_map(
        on_device, mesh=fine, in_specs=placed, out_specs=P(PTS, None, ORB), check_vma=False
    )
```
